32 devices in a mesh: dp: 8 (over z, x), mp: 4 (over y, core).
Axes of the slice: x: 2, y: 2, z: 4, core: 2. Of those that a mesh axis runs over, the one named last changes fastest.
Arguments:
- mel_frames: float32 [16384, 80], P('dp')
- frame_mask: int32 [8, 1024], replicated, may hold values from 0 to 1, as said below
- token_ids: int32 [8, 384], replicated, may hold values from 0 to 51839
- token_mask: int32 [8, 384], replicated, may hold values from 0 to 1, as said below
- embedding: float32 [51840, 768], P('dp', 'mp'), may hold values from -6 to 6
- conv_one: float32 [3, 80, 768], P(None, None, ('dp', 'mp')), may hold values from -0.375 to 0.375
- conv_two: float32 [3, 768, 768], P(None, ('dp', 'mp')), may hold values from -0.125 to 0.125
- enc_qkv: float32 [3, 768, 768], P(None, 'dp', 'mp'), may hold values from -0.21875 to 0.21875
- enc_out: float32 [768, 768], P('mp', 'dp'), may hold values from -3.5 to 3.5
- enc_up: float32 [768, 3072], P('dp', 'mp'), may hold values from -0.21875 to 0.21875
- enc_down: float32 [3072, 768], P('mp', 'dp'), may hold values from -0.109375 to 0.109375
- cross_qkv: float32 [3, 768, 768], P(None, 'dp', 'mp'), may hold values from -0.21875 to 0.21875
- cross_out: float32 [768, 768], P('mp', 'dp'), may hold values from -3.5 to 3.5
- dec_qkv: float32 [3, 768, 768], P(None, 'dp', 'mp'), may hold values from -0.21875 to 0.21875
- dec_out: float32 [768, 768], P('mp', 'dp'), may hold values from -1.75 to 1.75
- dec_up: float32 [768, 3072], P('dp', 'mp'), may hold values from -0.21875 to 0.21875
- dec_down: float32 [3072, 768], P('mp', 'dp'), may hold values from -0.109375 to 0.109375
- norm_params: float32 [6, 2, 768], P(None, None, 'dp'), as said below
- cotangent: float32 [3072, 768], P('dp'), may hold values from -6 to 6
Outputs:
- decoded: float32 [3072, 768], P('dp')
- mel_grad: float32 [16384, 80], P('dp')
- embed_grad: float32 [51840, 768], P('dp', 'mp')
- conv_one_grad: float32 [3, 80, 768], P(None, None, ('dp', 'mp'))
- conv_two_grad: float32 [3, 768, 768], P(None, ('dp', 'mp'))
- enc_qkv_grad: float32 [3, 768, 768], P(None, 'dp', 'mp')
- enc_out_grad: float32 [768, 768], P('mp', 'dp')
- enc_up_grad: float32 [768, 3072], P('dp', 'mp')
- enc_down_grad: float32 [3072, 768], P('mp', 'dp')
- cross_qkv_grad: float32 [3, 768, 768], P(None, 'dp', 'mp')
- cross_out_grad: float32 [768, 768], P('mp', 'dp')
- dec_qkv_grad: float32 [3, 768, 768], P(None, 'dp', 'mp')
- dec_out_grad: float32 [768, 768], P('mp', 'dp')
- dec_up_grad: float32 [768, 3072], P('dp', 'mp')
- dec_down_grad: float32 [3072, 768], P('mp', 'dp')
- norm_grad: float32 [6, 2, 768], P(None, None, 'dp')
- rms_stats: float32 [9], replicated
The draws below stay inside these ranges and needn't reach their ends.
Inputs may be any that keep to these rules, and one draw needn't show every extreme that they name: `frame_mask`: each clip's row is 1 on a prefix of at least max(68, 1) frames and 0 after it; some clip is valid in full. `token_mask`: each clip's row is 1 on a prefix of at least max(24, 1) tokens and 0 after it; some clip is valid in full. `norm_params`: gains near one and biases near zero.
All inputs are finite; a program needn't handle non-finite values.
Results may differ from the reference program's by a relative error of at most 0.0003.
Values sent between devices are 32-bit elements; how exact they have to be, the bound alone decides.
A program may use at most 256 MiB of HBM per device.

```python
import math
import jax
import jax.numpy as jnp
import numpy as np
from jax import lax

D = 768
HEAD = 64
FF = 3072
MEL = 80
VOCAB = 51840
FR = 512
TOK = 192
CLIPS = 8


def draw_mel_frames(key, part):
    total_rows = CLIPS * 4 * FR
    clip_of = jnp.arange(total_rows) // (4 * FR)
    ramp = jnp.exp(math.log(3.0) * clip_of.astype(jnp.float32) / max(CLIPS - 1, 1))
    base = jnp.clip(jax.random.normal(key, (total_rows, MEL), jnp.float32), -4.0, 4.0)
    return base * ramp[:, None]


def prefix_mask(key, most, least):
    lengths = jax.random.randint(jax.random.fold_in(key, 11), (CLIPS,), least, most + 1)
    full_clip = jax.random.randint(jax.random.fold_in(key, 12), (), 0, CLIPS)
    lengths = jnp.where(jnp.arange(CLIPS) == full_clip, most, lengths)
    return (jnp.arange(most)[None, :] < lengths[:, None]).astype(jnp.int32)


def draw_frame_mask(key, part):
    return prefix_mask(key, 2 * FR, max(2 * FR // 15, 1))


def draw_token_mask(key, part):
    return prefix_mask(key, 2 * TOK, max(2 * TOK // 16, 1))


def draw_norm_params(key, part):
    gain_key = jax.random.fold_in(key, 21)
    bias_key = jax.random.fold_in(key, 22)
    gains = 1.0 + 0.15 * jnp.clip(jax.random.normal(gain_key, (6, D), jnp.float32), -3.0, 3.0)
    biases = 0.3 * jnp.clip(jax.random.normal(bias_key, (6, D), jnp.float32), -3.0, 3.0)
    return jnp.stack([gains, biases], axis=1)


def place_ends(entries, own_key, smallest, high):
    extent = entries.shape
    spot = [jax.random.randint(jax.random.fold_in(own_key, axis), (), 0, extent[axis]) for axis in range(len(extent))]
    entries = entries.at[tuple(spot)].set(smallest)
    longest = extent.index(max(extent))
    spot[longest] = (spot[longest] + 1) % extent[longest]
    return entries.at[tuple(spot)].set(high)


def steps_of(stream_key, shape, split, smallest, largest):
    def one(dim, shards_of):
        draws = jax.random.uniform(jax.random.fold_in(jax.random.fold_in(stream_key, 6), dim), (shards_of,), jnp.float32, smallest / len(split), largest / len(split))
        return jnp.repeat(jnp.exp(draws), shape[dim] // shards_of).reshape((-1,) + (1,) * (len(shape) - dim - 1))

    loudness = one(*split[0])
    for cut in split[1:]:
        loudness = loudness * one(*cut)
    return loudness


def rank_bounds(number_of, lean):
    portions = [(1 << 20) // math.isqrt(grade ** lean) + 1 for grade in range(1, number_of + 1)]
    scale = 1 + sum(portions) // (1 << 30)
    return np.cumsum(np.array([max(1, weight // scale) for weight in portions]))


def ranked_ids(rng, dims, amount, lean):
    table = rank_bounds(amount, lean)
    ticket = jax.random.randint(jax.random.fold_in(rng, 1), dims, 0, int(table[amount - 1]))
    rank = jnp.searchsorted(jnp.asarray(table, jnp.int32), ticket, side="right")
    return jax.random.permutation(jax.random.fold_in(rng, 2), amount)[rank].astype(jnp.int32)


def centred(stream_key, dims, width, bound, pieces=(), held_as=jnp.bfloat16):
    gain = steps_of(stream_key, dims, pieces, -0.22, 0.18) if pieces else 1.0
    drawn = jax.random.normal(stream_key, dims, jnp.float32) * width * gain
    return jnp.minimum(jnp.maximum(drawn, -bound), bound).astype(held_as)


def setup_inputs(seed: int = 0) -> dict:
    seeds = jax.random.split(jax.random.key(seed), 20)
    return {
        "mel_frames": draw_mel_frames(jax.random.fold_in(seeds[19], 71), 0),
        "frame_mask": draw_frame_mask(jax.random.fold_in(seeds[19], 71), 0),
        "token_ids": place_ends(ranked_ids(seeds[2], (CLIPS, 2 * TOK), VOCAB, 2), jax.random.fold_in(seeds[2], 3), 0, VOCAB - 1).astype(jnp.int32),
        "token_mask": draw_token_mask(jax.random.fold_in(seeds[19], 71), 0),
        "embedding": centred(seeds[4], (VOCAB, D), 1.0, 6.0, ((0, 8), (1, 4)), jnp.float32),
        "conv_one": centred(seeds[5], (3, MEL, D), (3 * MEL) ** -0.5, 0.375, ((2, 32),), jnp.float32),
        "conv_two": centred(seeds[6], (3, D, D), (3 * D) ** -0.5, 0.125, ((1, 32),), jnp.float32),
        "enc_qkv": centred(seeds[7], (3, D, D), D ** -0.5, 0.21875, ((1, 8), (2, 4)), jnp.float32),
        "enc_out": centred(seeds[8], (D, D), (max(D // 256, 1)) ** -0.5, 3.5, ((0, 4), (1, 8)), jnp.float32),
        "enc_up": centred(seeds[9], (D, FF), D ** -0.5, 0.21875, ((0, 8), (1, 4)), jnp.float32),
        "enc_down": centred(seeds[10], (FF, D), FF ** -0.5, 0.109375, ((0, 4), (1, 8)), jnp.float32),
        "cross_qkv": centred(seeds[11], (3, D, D), D ** -0.5, 0.21875, ((1, 8), (2, 4)), jnp.float32),
        "cross_out": centred(seeds[12], (D, D), (max(D // 256, 1)) ** -0.5, 3.5, ((0, 4), (1, 8)), jnp.float32),
        "dec_qkv": centred(seeds[13], (3, D, D), D ** -0.5, 0.21875, ((1, 8), (2, 4)), jnp.float32),
        "dec_out": centred(seeds[14], (D, D), (max(D // 64, 1)) ** -0.5, 1.75, ((0, 4), (1, 8)), jnp.float32),
        "dec_up": centred(seeds[15], (D, FF), D ** -0.5, 0.21875, ((0, 8), (1, 4)), jnp.float32),
        "dec_down": centred(seeds[16], (FF, D), FF ** -0.5, 0.109375, ((0, 4), (1, 8)), jnp.float32),
        "norm_params": draw_norm_params(jax.random.fold_in(seeds[19], 71), 0),
        "cotangent": centred(seeds[18], (CLIPS * 2 * TOK, D), 1.0, 6.0, ((0, 8),), jnp.float32),
    }


HIGH = lax.Precision.HIGHEST
NEG = -1e+30
EPS = 1e-05

@jax.custom_vjp
def low(v):
    return lax.optimization_barrier(v.astype(jnp.bfloat16)).astype(jnp.float32)

@jax.custom_vjp
def low_back(v):
    return v

def low_keep(v):
    return (low(v), None)

def low_pass(kept, grad):
    return (grad,)

def back_keep(v):
    return (v, None)

def back_low(kept, grad):
    return (low(grad),)
low.defvjp(low_keep, low_pass)
low_back.defvjp(back_keep, back_low)

def matmul(left, right):
    return jnp.dot(left, right, precision=HIGH, preferred_element_type=jnp.float32)

def gelu_exact(tensor):
    return jax.nn.gelu(tensor, approximate=False)

def layer_norm(tensor, norm_param):
    centre = tensor - lax.optimization_barrier(jnp.mean(tensor, axis=-1, keepdims=True))
    spread = lax.optimization_barrier(jnp.mean(centre * centre, axis=-1, keepdims=True))
    return centre * lax.rsqrt(spread + EPS) * norm_param[0] + norm_param[1]

def sinusoid(position, model_width):
    half_width = model_width // 2
    inverse_rates = jnp.exp(-math.log(10000.0) * jnp.arange(half_width).astype(jnp.float32) / (half_width - 1))
    angles = position.astype(jnp.float32)[:, None] * inverse_rates[None, :]
    return jnp.concatenate([jnp.sin(angles), jnp.cos(angles)], axis=1)

def split_heads(tensor):
    return tensor.reshape(tensor.shape[0], -1, HEAD)

def attention(source_query, source_keys, weights, out_weight, allowed):
    queries = split_heads(matmul(source_query, weights[0]))
    key_rows = split_heads(matmul(source_keys, weights[1]))
    values = split_heads(matmul(source_keys, weights[2]))
    scores = jnp.einsum('qhe,khe->hqk', queries, key_rows, precision=HIGH) / math.sqrt(HEAD)
    scores = jnp.where(allowed[None], scores, NEG)
    probs = jax.nn.softmax(scores, axis=-1)
    mixed = jnp.einsum('hqk,khe->qhe', probs, values, precision=HIGH)
    return matmul(mixed.reshape(mixed.shape[0], -1), out_weight)

def feed_forward(normed, up_weight, down_weight):
    return matmul(gelu_exact(matmul(normed, up_weight)), down_weight)

def masked_squares(tensor, row_weight):
    return jnp.sum(row_weight[:, None] * tensor * tensor)

def reference(mel_frames, frame_mask, token_ids, token_mask, embedding, conv_one, conv_two, enc_qkv, enc_out, enc_up, enc_down, cross_qkv, cross_out, dec_qkv, dec_out, dec_up, dec_down, norm_params, cotangent):

    def forward(mel_frames, embedding, conv_one, conv_two, enc_qkv, enc_out, enc_up, enc_down, cross_qkv, cross_out, dec_qkv, dec_out, dec_up, dec_down, norm_params):

        def one_clip(items):
            mel_clip, frame_flags, id_row, token_flags = items
            frame_ok = frame_flags > 0
            token_ok = token_flags > 0
            mel_rows = mel_clip.shape[0]
            padded = jnp.pad(mel_clip, ((1, 1), (0, 0)))
            stem_one = gelu_exact(matmul(padded[0:mel_rows], conv_one[0]) + matmul(padded[1:mel_rows + 1], conv_one[1]) + matmul(padded[2:mel_rows + 2], conv_one[2]))
            padded_one = jnp.pad(stem_one, ((1, 1), (0, 0)))
            stem_two = matmul(padded_one[0:mel_rows:2], conv_two[0]) + matmul(padded_one[1:mel_rows + 1:2], conv_two[1]) + matmul(padded_one[2:mel_rows + 2:2], conv_two[2])
            enc_rows = mel_rows // 2
            stream_zero = gelu_exact(stem_two) + sinusoid(jnp.arange(enc_rows), D)
            enc_allowed = jnp.broadcast_to(frame_ok[None, :], (enc_rows, enc_rows))
            normed_stream = layer_norm(stream_zero, norm_params[0])
            enc_attn = attention(normed_stream, normed_stream, enc_qkv, enc_out, enc_allowed)
            stream_one = stream_zero + enc_attn
            enc_mlp = feed_forward(layer_norm(stream_one, norm_params[1]), enc_up, enc_down)
            stream_two = stream_one + enc_mlp
            memory = layer_norm(stream_two, norm_params[2])
            text_rows = id_row.shape[0]
            text_zero = jnp.take(embedding, id_row, axis=0) + sinusoid(jnp.arange(text_rows), D)
            positions = jnp.arange(text_rows)
            self_allowed = (positions[None, :] <= positions[:, None]) & token_ok[None, :]
            normed_text = layer_norm(text_zero, norm_params[3])
            dec_attn = attention(normed_text, normed_text, dec_qkv, dec_out, self_allowed)
            text_one = text_zero + dec_attn
            cross_allowed = jnp.broadcast_to(frame_ok[None, :], (text_rows, enc_rows))
            cross_attn = attention(layer_norm(text_one, norm_params[4]), memory, cross_qkv, cross_out, cross_allowed)
            text_two = text_one + cross_attn
            dec_mlp = feed_forward(layer_norm(text_two, norm_params[5]), dec_up, dec_down)
            decoded = text_two + dec_mlp
            frame_weight = frame_ok.astype(jnp.float32)
            token_weight = token_ok.astype(jnp.float32)
            square_sums = jnp.stack([masked_squares(stream_zero, frame_weight), masked_squares(enc_attn, frame_weight), masked_squares(enc_mlp, frame_weight), masked_squares(stream_two, frame_weight), masked_squares(text_zero, token_weight), masked_squares(dec_attn, token_weight), masked_squares(cross_attn, token_weight), masked_squares(dec_mlp, token_weight), masked_squares(decoded, token_weight)])
            return (decoded, square_sums)
        outputs, sums_all = lax.map(jax.checkpoint(one_clip), (mel_frames.reshape(CLIPS, 4 * FR, MEL), frame_mask, token_ids, token_mask))
        return (outputs.reshape(CLIPS * 2 * TOK, D), lax.optimization_barrier(jnp.sum(sums_all, axis=0)))
    floats = (mel_frames, embedding, conv_one, conv_two, enc_qkv, enc_out, enc_up, enc_down, cross_qkv, cross_out, dec_qkv, dec_out, dec_up, dec_down, norm_params)
    decoded, pull, square_sums = jax.vjp(forward, *floats, has_aux=True)
    grads = pull(cotangent)
    frame_total = jnp.sum(frame_mask).astype(jnp.float32)
    token_total = jnp.sum(token_mask).astype(jnp.float32)
    counts = jnp.stack([frame_total, frame_total, frame_total, frame_total, token_total, token_total, token_total, token_total, token_total])
    rms_stats = jnp.sqrt(square_sums / (counts * D))
    return (decoded, grads[0], grads[1], grads[2], grads[3], grads[4], grads[5], grads[6], grads[7], grads[8], grads[9], grads[10], grads[11], grads[12], grads[13], grads[14], rms_stats)
```

```python
import functools
import math

import jax
import jax.numpy as jnp
from jax import lax
from jax.experimental import pallas as pl
from jax.experimental.pallas import tpu as pltpu
from jax.sharding import PartitionSpec as P

HEAD = 64
HIGH = lax.Precision.HIGH
NEG = -1e30
EPS = 1e-05
RSQRT2 = 1.0 / math.sqrt(2.0)
RSQRT2PI = 1.0 / math.sqrt(2.0 * math.pi)


def dot(left, right, contract):
    return lax.dot_general(
        left, right, (contract, ((), ())), precision=HIGH, preferred_element_type=jnp.float32
    )


def mm(left, right):
    return dot(left, right, ((1,), (0,)))


def mm_nt(left, right):
    return dot(left, right, ((1,), (1,)))


def mm_tn(left, right):
    return dot(left, right, ((0,), (0,)))


def gelu(v):
    return 0.5 * v * (1.0 + lax.erf(v * RSQRT2))


def gelu_slope(v):
    return 0.5 * (1.0 + lax.erf(v * RSQRT2)) + v * (RSQRT2PI * jnp.exp(-0.5 * v * v))


def normalize(rows):
    centre = rows - jnp.mean(rows, axis=-1, keepdims=True)
    scale = lax.rsqrt(jnp.mean(centre * centre, axis=-1, keepdims=True) + EPS)
    return centre * scale, scale


def norm_back(grad, xhat, scale, gain):
    inner = grad * gain
    return (
        inner
        - jnp.mean(inner, axis=-1, keepdims=True)
        - xhat * jnp.mean(inner * xhat, axis=-1, keepdims=True)
    ) * scale


def exchange(value, axis, flip):
    size = lax.axis_size(axis)
    return lax.ppermute(value, axis, [(i, i ^ flip) for i in range(size)])


def model_sum(part):
    if lax.axis_size("mp") != 4:
        raise ValueError("mp size")
    half = part.shape[0] // 2
    pair = part[:half] + exchange(part[half:], "mp", 1)
    total = pair + exchange(pair, "mp", 2)
    return jnp.concatenate([total, exchange(total, "mp", 1)], axis=0)


def place_pieces(pieces):
    count = len(pieces)
    rows, width = pieces[0].shape

    def kernel(*refs):
        out = refs[count]
        place = lax.axis_index("dp")
        for flip in range(count):
            out[jnp.bitwise_xor(place, flip)] = refs[flip][...]

    size = count * rows * width * 4
    return pl.pallas_call(
        kernel,
        out_shape=jax.ShapeDtypeStruct((count, rows, width), jnp.float32),
        in_specs=[pl.BlockSpec(memory_space=pltpu.VMEM)] * count,
        out_specs=pl.BlockSpec(memory_space=pltpu.VMEM),
        cost_estimate=pl.CostEstimate(flops=0, bytes_accessed=2 * size, transcendentals=0),
        name="place_pieces",
    )(*pieces)


def gather_data(shard):
    count = lax.axis_size("dp")
    if count > 8:
        return lax.all_gather(shard, "dp", axis=0, tiled=False)
    pieces = [None] * count
    pieces[0] = shard
    for flip in range(2, count, 2):
        pieces[flip] = exchange(shard, "dp", flip)
    for flip in range(0, count, 2):
        pieces[flip + 1] = exchange(pieces[flip], "dp", 1)
    return place_pieces(pieces)


def scatter_data(blocks):
    count = lax.axis_size("dp")
    if count > 8:
        return lax.psum_scatter(blocks, "dp", scatter_dimension=0, tiled=False)
    place = lax.axis_index("dp")
    high, low = place // 2, place % 2
    grouped = blocks.reshape((count // 2, 2) + blocks.shape[1:])
    away = lax.dynamic_index_in_dim(grouped, 1 - low, 1, keepdims=False)
    kept = lax.dynamic_index_in_dim(grouped, low, 1, keepdims=False)
    pair = kept + exchange(away, "dp", 1)
    total = lax.dynamic_index_in_dim(pair, high, 0, keepdims=False)
    for flip in range(1, count // 2):
        piece = lax.dynamic_index_in_dim(pair, high ^ flip, 0, keepdims=False)
        total = total + exchange(piece, "dp", 2 * flip)
    return total


def data_sum(value):
    count = lax.axis_size("dp")
    if count > 8:
        return lax.psum(value, "dp")
    flip = 1
    while flip < count:
        value = value + exchange(value, "dp", flip)
        flip *= 2
    return value


def split_heads(rows):
    return rows.reshape(rows.shape[0], -1, HEAD)


def attend(queries, keys, values, allowed):
    factor = 1.0 / math.sqrt(HEAD)
    q, k, v = split_heads(queries), split_heads(keys), split_heads(values)
    scores = jnp.einsum("qhe,khe->hqk", q, k, precision=HIGH) * factor
    scores = jnp.where(allowed[None], scores, NEG)
    peaks = jnp.max(scores, axis=-1, keepdims=True)
    weight = jnp.exp(scores - peaks)
    totals = jnp.sum(weight, axis=-1, keepdims=True)
    output = jnp.einsum("hqk,khe->qhe", weight / totals, v, precision=HIGH)
    return output.reshape(queries.shape), peaks + jnp.log(totals)


def attend_back(queries, keys, values, allowed, output, log_total, grad):
    factor = 1.0 / math.sqrt(HEAD)
    q, k, v = split_heads(queries), split_heads(keys), split_heads(values)
    grad_out, out = split_heads(grad), split_heads(output)
    scores = jnp.einsum("qhe,khe->hqk", q, k, precision=HIGH) * factor
    probs = jnp.where(allowed[None], jnp.exp(scores - log_total), 0.0)
    grad_v = jnp.einsum("hqk,qhe->khe", probs, grad_out, precision=HIGH)
    grad_p = jnp.einsum("qhe,khe->hqk", grad_out, v, precision=HIGH)
    inner = jnp.sum(grad_out * out, axis=-1)
    grad_s = probs * (grad_p - inner.T[:, :, None]) * factor
    grad_q = jnp.einsum("hqk,khe->qhe", grad_s, k, precision=HIGH)
    grad_k = jnp.einsum("hqk,qhe->khe", grad_s, q, precision=HIGH)
    return (
        grad_q.reshape(queries.shape),
        grad_k.reshape(keys.shape),
        grad_v.reshape(values.shape),
    )


def rows_of(flat, width):
    flat = flat.reshape(-1)
    short = -flat.shape[0] % width
    return jnp.pad(flat, (0, short)).reshape(-1, width)


def pad_rows(rows):
    return jnp.pad(rows, ((0, -rows.shape[0] % 8), (0, 0)))


def attn_pack(weight, out_weight):
    return jnp.concatenate([weight[0], weight[1], weight[2], out_weight.T], axis=1)


def body(
    mel_frames,
    frame_mask,
    token_ids,
    token_mask,
    embedding,
    conv_one,
    conv_two,
    enc_qkv,
    enc_out,
    enc_up,
    enc_down,
    cross_qkv,
    cross_out,
    dec_qkv,
    dec_out,
    dec_up,
    dec_down,
    norm_params,
    cotangent,
):
    n_dp = lax.axis_size("dp")
    dp_place, mp_place = lax.axis_index("dp"), lax.axis_index("mp")
    turned = (mp_place % 2) == 1
    frames = mel_frames.shape[0] // 2
    mel = mel_frames.shape[1]
    tokens, width = cotangent.shape
    local = enc_qkv.shape[2]
    taps, chans = conv_one.shape[0], conv_one.shape[2]

    def turn(rows):
        half = rows.shape[0] // 2
        return jnp.where(turned, jnp.concatenate([rows[half:], rows[:half]], axis=0), rows)

    def positions(count):
        index = lax.broadcasted_iota(jnp.int32, (count, 1), 0)
        return jnp.where(turned, jnp.where(index >= count // 2, index - count // 2, index + count // 2), index)

    def sinusoid(count):
        half_width = width // 2
        rates = jnp.exp(-math.log(10000.0) * jnp.arange(half_width).astype(jnp.float32) / (half_width - 1))
        angles = positions(count).astype(jnp.float32) * rates[None, :]
        return jnp.concatenate([jnp.sin(angles), jnp.cos(angles)], axis=1)

    conv_rows = pad_rows(
        jnp.concatenate(
            [
                conv_two.reshape(-1, width),
                rows_of(conv_one.transpose(2, 0, 1), width),
                rows_of(norm_params, width),
            ],
            axis=0,
        )
    )
    stem_all = gather_data(conv_rows)
    enc_attn_all = gather_data(attn_pack(enc_qkv, enc_out)).reshape(width, -1)
    dec_attn_all = gather_data(attn_pack(dec_qkv, dec_out)).reshape(width, -1)
    enc_mlp_all = gather_data(jnp.concatenate([enc_up, enc_down.T], axis=0))
    cross_all = gather_data(attn_pack(cross_qkv, cross_out)).reshape(width, -1)
    dec_mlp_all = gather_data(jnp.concatenate([dec_up, dec_down.T], axis=0))

    part = width // n_dp
    two_rows = taps * chans
    one_size = taps * mel * chans
    one_rows = -(-one_size // width)
    stem_width = n_dp * chans
    w_two = (
        stem_all[:, :two_rows]
        .reshape(n_dp, taps, chans, width)
        .transpose(1, 0, 2, 3)
        .reshape(taps * stem_width, width)
    )
    w_one = (
        stem_all[:, two_rows : two_rows + one_rows]
        .reshape(n_dp, -1)[:, :one_size]
        .reshape(stem_width, taps * mel)
    )
    norms = (
        stem_all[:, two_rows + one_rows :]
        .reshape(n_dp, -1)[:, : 12 * part]
        .reshape(n_dp, 6, 2, part)
        .transpose(1, 2, 0, 3)
        .reshape(6, 2, width)
    )
    w_both = jnp.concatenate(
        [jnp.pad(w_one, ((0, 0), (0, mel))), jnp.pad(w_one, ((0, 0), (mel, 0)))], axis=0
    )
    ff = enc_up.shape[1]
    enc_up_all = enc_mlp_all[:, :part].reshape(width, ff)
    enc_down_all = enc_mlp_all[:, part:].reshape(width, ff)
    dec_up_all = dec_mlp_all[:, :part].reshape(width, ff)
    dec_down_all = dec_mlp_all[:, part:].reshape(width, ff)

    frame_row = lax.dynamic_index_in_dim(frame_mask, dp_place, 0, keepdims=False) > 0
    token_row = lax.dynamic_index_in_dim(token_mask, dp_place, 0, keepdims=False) > 0
    frame_ok, token_ok = turn(frame_row), turn(token_row)
    frame_allowed = frame_ok[None, :]
    text_at = positions(tokens)
    self_allowed = (text_at.reshape(1, -1) <= text_at) & token_ok[None, :]
    cot = turn(cotangent)

    frame_at = positions(frames)
    first, last = frame_at == 0, frame_at == frames - 1
    both = turn(mel_frames.reshape(frames, 2 * mel))
    before = jnp.where(first, 0.0, jnp.roll(both[:, mel:], 1, axis=0))
    after = jnp.where(last, 0.0, jnp.roll(both[:, :mel], -1, axis=0))
    window = jnp.concatenate([before, both, after], axis=1)
    pre_one = mm_nt(window, w_both)
    stem_one = gelu(pre_one)
    odd = stem_one[:, stem_width:]
    stem_cat = jnp.concatenate([jnp.where(first, 0.0, jnp.roll(odd, 1, axis=0)), stem_one], axis=1)
    stem_sum = model_sum(mm(stem_cat, w_two))
    stream_zero = gelu(stem_sum) + sinusoid(frames)

    hat_zero, scale_zero = normalize(stream_zero)
    ln_zero = hat_zero * norms[0, 0] + norms[0, 1]
    enc_three = mm(ln_zero, enc_attn_all[:, : 3 * local])
    enc_q, enc_k, enc_v = (enc_three[:, i * local : (i + 1) * local] for i in range(3))
    enc_mixed, enc_lse = attend(enc_q, enc_k, enc_v, frame_allowed)
    enc_attn = model_sum(mm_nt(enc_mixed, enc_attn_all[:, 3 * local :]))
    stream_one = stream_zero + enc_attn
    hat_one, scale_one = normalize(stream_one)
    ln_one = hat_one * norms[1, 0] + norms[1, 1]
    enc_pre = mm(ln_one, enc_up_all)
    enc_hidden = gelu(enc_pre)
    enc_mlp = model_sum(mm_nt(enc_hidden, enc_down_all))
    stream_two = stream_one + enc_mlp
    hat_two, scale_two = normalize(stream_two)
    memory = hat_two * norms[2, 0] + norms[2, 1]
    cross_two = mm(memory, cross_all[:, local : 3 * local])
    cross_k, cross_v = cross_two[:, :local], cross_two[:, local:]

    vocab_rows, embed_width = embedding.shape
    local_ids = token_ids.reshape(-1) - dp_place * vocab_rows
    owned = (local_ids >= 0) & (local_ids < vocab_rows)
    safe_ids = jnp.clip(local_ids, 0, vocab_rows - 1)
    picked = jnp.where(owned[:, None], jnp.take(embedding, safe_ids, axis=0), 0.0)
    share = lax.psum_scatter(picked, "dp", scatter_dimension=0, tiled=True)
    text_zero = turn(lax.all_gather(share, "mp", axis=1, tiled=True)) + sinusoid(tokens)

    hat_three, scale_three = normalize(text_zero)
    ln_three = hat_three * norms[3, 0] + norms[3, 1]
    dec_three = mm(ln_three, dec_attn_all[:, : 3 * local])
    dec_q, dec_k, dec_v = (dec_three[:, i * local : (i + 1) * local] for i in range(3))
    dec_mixed, dec_lse = attend(dec_q, dec_k, dec_v, self_allowed)
    dec_attn = model_sum(mm_nt(dec_mixed, dec_attn_all[:, 3 * local :]))
    text_one = text_zero + dec_attn
    hat_four, scale_four = normalize(text_one)
    ln_four = hat_four * norms[4, 0] + norms[4, 1]
    cross_q = mm(ln_four, cross_all[:, :local])
    cross_mixed, cross_lse = attend(cross_q, cross_k, cross_v, frame_allowed)
    cross_attn = model_sum(mm_nt(cross_mixed, cross_all[:, 3 * local :]))
    text_two = text_one + cross_attn
    hat_five, scale_five = normalize(text_two)
    ln_five = hat_five * norms[5, 0] + norms[5, 1]
    dec_pre = mm(ln_five, dec_up_all)
    dec_hidden = gelu(dec_pre)
    dec_mlp = model_sum(mm_nt(dec_hidden, dec_down_all))
    decoded = text_two + dec_mlp

    def half_of(rows):
        return rows[: rows.shape[0] // 2]

    frame_weight = half_of(frame_ok).astype(jnp.float32)[:, None]
    token_weight = half_of(token_ok).astype(jnp.float32)[:, None]

    def squares(rows, weight):
        kept = half_of(rows)
        return jnp.sum(kept * kept * weight)

    local_sums = jnp.stack(
        [squares(x, frame_weight) for x in (stream_zero, enc_attn, enc_mlp, stream_two)]
        + [squares(x, token_weight) for x in (text_zero, dec_attn, cross_attn, dec_mlp, decoded)]
    )
    local_sums = local_sums + exchange(local_sums, "mp", 1)
    square_sums = data_sum(local_sums)
    frame_total = jnp.sum((frame_mask > 0).astype(jnp.float32))
    token_total = jnp.sum((token_mask > 0).astype(jnp.float32))
    counts = jnp.concatenate([jnp.full((4,), frame_total), jnp.full((5,), token_total)])
    rms_stats = jnp.sqrt(square_sums / (counts * width))

    def norm_grads(grad, xhat):
        kept = half_of(grad)
        return jnp.stack([jnp.sum(kept * half_of(xhat), axis=0), jnp.sum(kept, axis=0)])

    def block(grad):
        return grad.reshape(n_dp, grad.shape[0] // n_dp, grad.shape[1])

    grad_dec_down = scatter_data(block(mm_tn(cot, dec_hidden)))
    grad_pre = mm(cot, dec_down_all) * gelu_slope(dec_pre)
    grad_dec_up = scatter_data(block(mm_tn(ln_five, grad_pre)))
    grad_ln = model_sum(mm_nt(grad_pre, dec_up_all))
    norm_five = norm_grads(grad_ln, hat_five)
    grad_text_two = cot + norm_back(grad_ln, hat_five, scale_five, norms[5, 0])

    grad_cross_out = mm_tn(grad_text_two, cross_mixed)
    grad_cq, grad_ck, grad_cv = attend_back(
        cross_q,
        cross_k,
        cross_v,
        frame_allowed,
        cross_mixed,
        cross_lse,
        mm(grad_text_two, cross_all[:, 3 * local :]),
    )
    grad_ckv = jnp.concatenate([grad_ck, grad_cv], axis=1)
    grad_cross = scatter_data(
        block(
            jnp.concatenate([mm_tn(ln_four, grad_cq), mm_tn(memory, grad_ckv), grad_cross_out], axis=1)
        )
    )
    grad_memory = model_sum(mm_nt(grad_ckv, cross_all[:, local : 3 * local]))
    grad_ln = model_sum(mm_nt(grad_cq, cross_all[:, :local]))
    norm_four = norm_grads(grad_ln, hat_four)
    grad_text_one = grad_text_two + norm_back(grad_ln, hat_four, scale_four, norms[4, 0])

    grad_dec_out = mm_tn(grad_text_one, dec_mixed)
    grad_three = jnp.concatenate(
        attend_back(
            dec_q,
            dec_k,
            dec_v,
            self_allowed,
            dec_mixed,
            dec_lse,
            mm(grad_text_one, dec_attn_all[:, 3 * local :]),
        ),
        axis=1,
    )
    grad_dec_attn = scatter_data(
        block(jnp.concatenate([mm_tn(ln_three, grad_three), grad_dec_out], axis=1))
    )
    grad_ln = model_sum(mm_nt(grad_three, dec_attn_all[:, : 3 * local]))
    norm_three = norm_grads(grad_ln, hat_three)
    grad_text_zero = grad_text_one + norm_back(grad_ln, hat_three, scale_three, norms[3, 0])
    grad_share = lax.dynamic_slice_in_dim(turn(grad_text_zero), mp_place * embed_width, embed_width, 1)
    grad_rows = lax.all_gather(grad_share, "dp", axis=0, tiled=True)
    grad_embedding = (
        jnp.zeros(embedding.shape, jnp.float32)
        .at[safe_ids]
        .add(jnp.where(owned[:, None], grad_rows, 0.0))
    )

    norm_two = norm_grads(grad_memory, hat_two)
    grad_stream_two = norm_back(grad_memory, hat_two, scale_two, norms[2, 0])
    grad_enc_down = scatter_data(block(mm_tn(grad_stream_two, enc_hidden)))
    grad_pre = mm(grad_stream_two, enc_down_all) * gelu_slope(enc_pre)
    grad_enc_up = scatter_data(block(mm_tn(ln_one, grad_pre)))
    grad_ln = model_sum(mm_nt(grad_pre, enc_up_all))
    norm_one = norm_grads(grad_ln, hat_one)
    grad_stream_one = grad_stream_two + norm_back(grad_ln, hat_one, scale_one, norms[1, 0])

    grad_enc_out = mm_tn(grad_stream_one, enc_mixed)
    grad_three = jnp.concatenate(
        attend_back(
            enc_q,
            enc_k,
            enc_v,
            frame_allowed,
            enc_mixed,
            enc_lse,
            mm(grad_stream_one, enc_attn_all[:, 3 * local :]),
        ),
        axis=1,
    )
    grad_enc_attn = scatter_data(
        block(jnp.concatenate([mm_tn(ln_zero, grad_three), grad_enc_out], axis=1))
    )
    grad_ln = model_sum(mm_nt(grad_three, enc_attn_all[:, : 3 * local]))
    norm_zero = norm_grads(grad_ln, hat_zero)
    grad_stream_zero = grad_stream_one + norm_back(grad_ln, hat_zero, scale_zero, norms[0, 0])

    grad_stem = grad_stream_zero * gelu_slope(stem_sum)
    grad_w_two = mm_tn(stem_cat, grad_stem)
    grad_cat = mm_nt(grad_stem, w_two)
    grad_back = jnp.roll(jnp.where(first, 0.0, grad_cat[:, :stem_width]), -1, axis=0)
    grad_one = jnp.concatenate(
        [grad_cat[:, stem_width : 2 * stem_width], grad_cat[:, 2 * stem_width :] + grad_back], axis=1
    )
    grad_pre = grad_one * gelu_slope(pre_one)
    grad_both = mm_tn(grad_pre, window)
    grad_w_one = grad_both[:stem_width, : taps * mel] + grad_both[stem_width:, mel:]
    grad_window = mm(grad_pre, w_both)
    grad_mel = grad_window[:, mel : 3 * mel] + jnp.concatenate(
        [
            jnp.roll(jnp.where(last, 0.0, grad_window[:, 3 * mel :]), 1, axis=0),
            jnp.roll(jnp.where(first, 0.0, grad_window[:, :mel]), -1, axis=0),
        ],
        axis=1,
    )
    grad_mel = turn(model_sum(grad_mel)).reshape(mel_frames.shape)

    norm_all = jnp.stack([norm_zero, norm_one, norm_two, norm_three, norm_four, norm_five])
    norm_all = norm_all + exchange(norm_all, "mp", 1)
    norm_blocks = norm_all.reshape(12, n_dp, part).transpose(1, 0, 2).reshape(n_dp, -1)
    one_blocks = grad_w_one.reshape(n_dp, one_size)

    def lay(flat):
        short = -flat.shape[1] % width
        return jnp.pad(flat, ((0, 0), (0, short))).reshape(n_dp, -1, width)

    two_blocks = (
        grad_w_two.reshape(taps, n_dp, chans, width).transpose(1, 0, 2, 3).reshape(n_dp, -1, width)
    )
    stem_blocks = jnp.concatenate([two_blocks, lay(one_blocks), lay(norm_blocks)], axis=1)
    stem_blocks = jnp.pad(stem_blocks, ((0, 0), (0, -stem_blocks.shape[1] % 8), (0, 0)))
    stem_grads = scatter_data(stem_blocks)
    grad_conv_two = stem_grads[:two_rows].reshape(taps, chans, width)
    grad_conv_one = (
        stem_grads[two_rows : two_rows + one_rows]
        .reshape(-1)[:one_size]
        .reshape(chans, taps, mel)
        .transpose(1, 2, 0)
    )
    grad_norms = stem_grads[two_rows + one_rows :].reshape(-1)[: 12 * part].reshape(6, 2, part)

    def three(grads):
        return jnp.stack([grads[:, i * local : (i + 1) * local] for i in range(3)])

    return (
        turn(decoded),
        grad_mel,
        grad_embedding,
        grad_conv_one,
        grad_conv_two,
        three(grad_enc_attn),
        grad_enc_attn[:, 3 * local :].T,
        grad_enc_up,
        grad_enc_down.T,
        three(grad_cross),
        grad_cross[:, 3 * local :].T,
        three(grad_dec_attn),
        grad_dec_attn[:, 3 * local :].T,
        grad_dec_up,
        grad_dec_down.T,
        grad_norms,
        rms_stats,
    )


def solution(mesh):
    placed = (
        P("dp", None),
        P(),
        P(),
        P(),
        P("dp", "mp"),
        P(None, None, ("dp", "mp")),
        P(None, ("dp", "mp"), None),
        P(None, "dp", "mp"),
        P("mp", "dp"),
        P("dp", "mp"),
        P("mp", "dp"),
        P(None, "dp", "mp"),
        P("mp", "dp"),
        P(None, "dp", "mp"),
        P("mp", "dp"),
        P("dp", "mp"),
        P("mp", "dp"),
        P(None, None, "dp"),
        P("dp", None),
    )
    return jax.shard_map(
        body,
        mesh=mesh,
        in_specs=placed,
        out_specs=(
            P("dp", None),
            P("dp", None),
            P("dp", "mp"),
            P(None, None, ("dp", "mp")),
            P(None, ("dp", "mp"), None),
            P(None, "dp", "mp"),
            P("mp", "dp"),
            P("dp", "mp"),
            P("mp", "dp"),
            P(None, "dp", "mp"),
            P("mp", "dp"),
            P(None, "dp", "mp"),
            P("mp", "dp"),
            P("dp", "mp"),
            P("mp", "dp"),
            P(None, None, "dp"),
            P(),
        ),
        check_vma=False,
    )
```

```python
import functools
import math

import jax
import jax.numpy as jnp
from jax import lax
from jax.experimental import pallas as pl
from jax.experimental.pallas import tpu as pltpu
from jax.sharding import PartitionSpec as P

HEAD = 64
HIGH = lax.Precision.HIGH
NEG = -1e30
EPS = 1e-05
RSQRT2 = 1.0 / math.sqrt(2.0)
RSQRT2PI = 1.0 / math.sqrt(2.0 * math.pi)


def dot(left, right, contract):
    return lax.dot_general(
        left, right, (contract, ((), ())), precision=HIGH, preferred_element_type=jnp.float32
    )


def mm(left, right):
    return dot(left, right, ((1,), (0,)))


def mm_nt(left, right):
    return dot(left, right, ((1,), (1,)))


def mm_tn(left, right):
    return dot(left, right, ((0,), (0,)))


def gelu(v):
    return 0.5 * v * (1.0 + lax.erf(v * RSQRT2))


def gelu_slope(v):
    return 0.5 * (1.0 + lax.erf(v * RSQRT2)) + v * (RSQRT2PI * jnp.exp(-0.5 * v * v))


def normalize(rows):
    centre = rows - jnp.mean(rows, axis=-1, keepdims=True)
    scale = lax.rsqrt(jnp.mean(centre * centre, axis=-1, keepdims=True) + EPS)
    return centre * scale, scale


def norm_back(grad, xhat, scale, gain):
    inner = grad * gain
    return (
        inner
        - jnp.mean(inner, axis=-1, keepdims=True)
        - xhat * jnp.mean(inner * xhat, axis=-1, keepdims=True)
    ) * scale


def exchange(value, axis, flip):
    size = lax.axis_size(axis)
    return lax.ppermute(value, axis, [(i, i ^ flip) for i in range(size)])


def model_sum(part):
    if lax.axis_size("mp") != 4:
        raise ValueError("mp size")
    half = part.shape[0] // 2
    pair = part[:half] + exchange(part[half:], "mp", 1)
    total = pair + exchange(pair, "mp", 2)
    return jnp.concatenate([total, exchange(total, "mp", 1)], axis=0)


def place_pieces(pieces):
    count = len(pieces)
    rows, width = pieces[0].shape

    def kernel(*refs):
        out = refs[count]
        place = lax.axis_index("dp")
        for flip in range(count):
            out[jnp.bitwise_xor(place, flip)] = refs[flip][...]

    size = count * rows * width * 4
    return pl.pallas_call(
        kernel,
        out_shape=jax.ShapeDtypeStruct((count, rows, width), jnp.float32),
        in_specs=[pl.BlockSpec(memory_space=pltpu.VMEM)] * count,
        out_specs=pl.BlockSpec(memory_space=pltpu.VMEM),
        cost_estimate=pl.CostEstimate(flops=0, bytes_accessed=2 * size, transcendentals=0),
        name="place_pieces",
    )(*pieces)


def gather_slow(shard):
    return lax.all_gather(shard, "dp", axis=0, tiled=False)


def split_rows(full, cuts):
    out = []
    for r0, r1, c0, c1 in cuts:
        x = full[:, r0:r1, c0:c1].reshape(full.shape[0] * (r1 - r0), c1 - c0)
        hi = lax.reduce_precision(x, 8, 7)
        out.append((hi.astype(BF), (x - hi).astype(BF)))
    return out


def scatter_slow(blocks):
    return lax.psum_scatter(blocks, "dp", scatter_dimension=0, tiled=False)


def tie(value, other):
    return lax.optimization_barrier((value, other))[0]


def gather_data(shard):
    count = lax.axis_size("dp")
    if count > 8:
        return lax.all_gather(shard, "dp", axis=0, tiled=False)
    return place_pieces(gather_pieces(shard))


def gather_pieces(shard):
    count = lax.axis_size("dp")
    pieces = [None] * count
    pieces[0] = shard
    for flip in range(2, count, 2):
        pieces[flip] = exchange(shard, "dp", flip)
    for flip in range(0, count, 2):
        pieces[flip + 1] = exchange(pieces[flip], "dp", 1)
    return pieces


def scatter_data(blocks):
    count = lax.axis_size("dp")
    if count > 8:
        return lax.psum_scatter(blocks, "dp", scatter_dimension=0, tiled=False)
    place = lax.axis_index("dp")
    high, low = place // 2, place % 2
    grouped = blocks.reshape((count // 2, 2) + blocks.shape[1:])
    away = lax.dynamic_index_in_dim(grouped, 1 - low, 1, keepdims=False)
    kept = lax.dynamic_index_in_dim(grouped, low, 1, keepdims=False)
    pair = kept + exchange(away, "dp", 1)
    total = lax.dynamic_index_in_dim(pair, high, 0, keepdims=False)
    for flip in range(1, count // 2):
        piece = lax.dynamic_index_in_dim(pair, high ^ flip, 0, keepdims=False)
        total = total + exchange(piece, "dp", 2 * flip)
    return total


def data_sum(value):
    count = lax.axis_size("dp")
    if count > 8:
        return lax.psum(value, "dp")
    flip = 1
    while flip < count:
        value = value + exchange(value, "dp", flip)
        flip *= 2
    return value


MESH = pl.DeviceIdType.MESH
BF = jnp.bfloat16
VMEM_LIMIT = 66_000_000
NN = ((1,), (0,))
NT = ((1,), (1,))
TN = ((0,), (0,))


def split(x):
    hi = x.astype(BF)
    return hi, (x - hi.astype(jnp.float32)).astype(BF)


def bdot(a, b, contract):
    return lax.dot_general(a, b, (contract, ((), ())), preferred_element_type=jnp.float32)


def dot3(a, b, contract):
    return bdot(a[0], b[0], contract) + (bdot(a[0], b[1], contract) + bdot(a[1], b[0], contract))


def take(pair, where):
    return pair[0][where], pair[1][where]


def rows_at(start, count):
    return (pl.ds(start if isinstance(start, int) else pl.multiple_of(start, 8), count), slice(None))


def put(pair, where, value):
    hi, lo = split(value)
    pair[0][where] = hi
    pair[1][where] = lo


def erf(x):
    x = jnp.clip(x, -3.832506856900711, 3.832506856900711)
    s = x * x
    num = s * 0.00022905065861350646 + 0.0034082910107109506
    num = num * s + 0.050955695062380861
    num = num * s + 0.18520832239976145
    num = num * s + 1.128379143519084
    den = s * -1.1791602954361697e-7 + 0.000023547966471313185
    den = den * s + 0.0010179625278914885
    den = den * s + 0.014070470171167667
    den = den * s + 0.11098505178285362
    den = den * s + 0.49746925110067538
    den = den * s + 1.0
    return x * num / den


def k_gelu(v):
    return 0.5 * v * (1.0 + erf(v * RSQRT2))


def k_slope(v):
    return 0.5 * (1.0 + erf(v * RSQRT2)) + v * (RSQRT2PI * jnp.exp(-0.5 * v * v))


class Links:
    def __init__(self, half, tm, bufs, sems):
        self.half, self.tm, self.n = half, tm, half // tm
        self.send_a, self.recv_a, self.send_b, self.recv_b, self.send_c, self.recv_c = bufs
        self.sems = sems
        place = lax.axis_index("mp")
        self.near = place + 1 - 2 * (place % 2)
        self.far = (place + 2) % 4

    def greet(self):
        barrier = pltpu.get_barrier_semaphore()
        for peer in (self.near, self.far):
            pl.semaphore_signal(barrier, inc=1, device_id={"mp": peer}, device_id_type=MESH)
        pl.semaphore_wait(barrier, 2)

    def copy(self, kind, i):
        src, dst, peer = (
            (self.send_a, self.recv_a, self.near),
            (self.send_b, self.recv_b, self.far),
            (self.send_c, self.recv_c, self.near),
        )[kind]
        part = pl.ds(i * self.tm, self.tm)
        return pltpu.make_async_remote_copy(
            src_ref=src.at[part],
            dst_ref=dst.at[part],
            send_sem=self.sems.at[2 * kind, i],
            recv_sem=self.sems.at[2 * kind + 1, i],
            device_id={"mp": peer},
            device_id_type=MESH,
        )

    def begin(self, part_of):
        for i in range(self.n):
            at = rows_at(i * self.tm, self.tm)
            self.send_a[at] = part_of(self.half + i * self.tm)
            self.copy(0, i).start()
            mine = part_of(i * self.tm)
            self.copy(0, i).wait_recv()
            self.send_b[at] = mine + self.recv_a[at]
            self.copy(1, i).start()

    def finish(self, done):
        for i in range(self.n):
            at = rows_at(i * self.tm, self.tm)
            self.copy(1, i).wait_recv()
            total = self.send_b[at] + self.recv_b[at]
            self.send_c[at] = total
            self.copy(2, i).start()
            done(i * self.tm, total, True)
        for i in range(self.n):
            self.copy(2, i).wait_recv()
            done(self.half + i * self.tm, self.recv_c[rows_at(i * self.tm, self.tm)], False)
        for kind in range(3):
            for i in range(self.n):
                self.copy(kind, i).wait_send()


def link_scratch(half, tm, width):
    return [pltpu.VMEM((half, width), jnp.float32)] * 6 + [pltpu.SemaphoreType.DMA((6, half // tm))]


def call(kernel, outs, ins, scratch, name, collective=None, flops=0):
    nbytes = sum(math.prod(x.shape) * x.dtype.itemsize for x in list(ins) + list(outs))
    return pl.pallas_call(
        kernel,
        out_shape=[jax.ShapeDtypeStruct(o.shape, o.dtype) for o in outs],
        in_specs=[pl.BlockSpec(memory_space=pltpu.VMEM)] * len(ins),
        out_specs=[pl.BlockSpec(memory_space=pltpu.VMEM)] * len(outs),
        scratch_shapes=scratch,
        compiler_params=pltpu.CompilerParams(
            vmem_limit_bytes=VMEM_LIMIT,
            collective_id=collective,
            has_side_effects=collective is not None,
        ),
        cost_estimate=pl.CostEstimate(flops=flops, bytes_accessed=nbytes, transcendentals=0),
        name=name,
    )(*ins)


def shape(*dims, dtype=jnp.float32):
    return jax.ShapeDtypeStruct(dims, dtype)


def row_stats(x):
    mean = jnp.mean(x, axis=-1, keepdims=True)
    centre = x - mean
    scale = lax.rsqrt(jnp.mean(centre * centre, axis=-1, keepdims=True) + EPS)
    return centre * scale, scale


def chunk_of(half):
    return 128 if half % 128 == 0 else half


def mlp_forward(x, norm, up, down, weight, collective, name):
    rows, width = x.shape
    ff = up[0].shape[1]
    half = rows // 2
    tm = chunk_of(half)

    def kernel(x_ref, norm_ref, uh, ul, dh, dl, w_ref, out, pre_out, stat, *rest):
        links = Links(half, tm, rest[:6], rest[6])
        links.greet()
        gain, bias = norm_ref[0:1, :], norm_ref[1:2, :]

        def part_of(start):
            at = rows_at(start, tm)
            hat, _ = row_stats(x_ref[at])
            pre = dot3(split(hat * gain + bias), (uh[...], ul[...]), NN)
            pre_out[at] = pre
            return dot3(split(k_gelu(pre)), (dh[...], dl[...]), NT)

        links.begin(part_of)
        stat[...] = jnp.zeros_like(stat)

        def done(start, total, mine):
            at = rows_at(start, tm)
            value = x_ref[at] + total
            out[at] = value
            if mine:
                w = w_ref[at]
                stat[0:1, :] += jnp.sum(total * total * w, axis=0, keepdims=True)
                stat[1:2, :] += jnp.sum(value * value * w, axis=0, keepdims=True)

        links.finish(done)

    return call(
        kernel,
        [shape(rows, width), shape(rows, ff), shape(8, width)],
        [x, norm, *up, *down, weight],
        link_scratch(half, tm, width),
        name,
        collective,
        flops=12 * rows * width * ff,
    )


def mlp_backward(grad, x, norm, pre, up, down, collective, name):
    rows, width = x.shape
    ff = up[0].shape[1]
    half = rows // 2
    tm = chunk_of(half)

    def kernel(g_ref, x_ref, norm_ref, pre_ref, uh, ul, dh, dl, out, dup, ddown, dnorm, lh, ll, ph, plo, hh, hl, gh, gl, *rest):
        links = Links(half, tm, rest[:6], rest[6])
        links.greet()
        gain, bias = norm_ref[0:1, :], norm_ref[1:2, :]

        def part_of(start):
            at = rows_at(start, tm)
            grad_rows = split(g_ref[at])
            gh[at], gl[at] = grad_rows
            pre_rows = pre_ref[at]
            cdf = 0.5 * (1.0 + erf(pre_rows * RSQRT2))
            put((hh, hl), at, pre_rows * cdf)
            slope = cdf + pre_rows * (RSQRT2PI * jnp.exp(-0.5 * pre_rows * pre_rows))
            grad_pre = split(dot3(grad_rows, (dh[...], dl[...]), NN) * slope)
            ph[at], plo[at] = grad_pre
            return dot3(grad_pre, (uh[...], ul[...]), NT)

        links.begin(part_of)

        for start in range(0, rows, tm):
            at = rows_at(start, tm)
            hat, _ = row_stats(x_ref[at])
            put((lh, ll), at, hat * gain + bias)
        step = 256 if width % 256 == 0 else width
        for c in range(0, width, step):
            cols = (slice(None), pl.ds(c, step))
            ddown[pl.ds(c, step), :] = dot3(take((gh, gl), cols), (hh[...], hl[...]), TN)
            dup[pl.ds(c, step), :] = dot3(take((lh, ll), cols), (ph[...], plo[...]), TN)
        dnorm[...] = jnp.zeros_like(dnorm)

        def done(start, total, mine):
            at = rows_at(start, tm)
            hat, scale = row_stats(x_ref[at])
            if mine:
                dnorm[0:1, :] += jnp.sum(total * hat, axis=0, keepdims=True)
                dnorm[1:2, :] += jnp.sum(total, axis=0, keepdims=True)
            out[at] = g_ref[at] + norm_back(total, hat, scale, gain)

        links.finish(done)

    return call(
        kernel,
        [shape(rows, width), shape(width, ff), shape(width, ff), shape(8, width)],
        [grad, x, norm, pre, *up, *down],
        [pltpu.VMEM((rows, width), BF)] * 2
        + [pltpu.VMEM((rows, ff), BF)] * 4
        + [pltpu.VMEM((rows, width), BF)] * 2
        + link_scratch(half, tm, width),
        name,
        collective,
        flops=24 * rows * width * ff,
    )


def split_heads(rows):
    return rows.reshape(rows.shape[0], -1, HEAD)


def attend(queries, keys, values, allowed):
    factor = 1.0 / math.sqrt(HEAD)
    q, k, v = split_heads(queries), split_heads(keys), split_heads(values)
    scores = jnp.einsum("qhe,khe->hqk", q, k, precision=HIGH) * factor
    scores = jnp.where(allowed[None], scores, NEG)
    peaks = jnp.max(scores, axis=-1, keepdims=True)
    weight = jnp.exp(scores - peaks)
    totals = jnp.sum(weight, axis=-1, keepdims=True)
    output = jnp.einsum("hqk,khe->qhe", weight / totals, v, precision=HIGH)
    return output.reshape(queries.shape), peaks + jnp.log(totals)


def attend_back(queries, keys, values, allowed, output, log_total, grad):
    factor = 1.0 / math.sqrt(HEAD)
    q, k, v = split_heads(queries), split_heads(keys), split_heads(values)
    grad_out, out = split_heads(grad), split_heads(output)
    scores = jnp.einsum("qhe,khe->hqk", q, k, precision=HIGH) * factor
    probs = jnp.where(allowed[None], jnp.exp(scores - log_total), 0.0)
    grad_v = jnp.einsum("hqk,qhe->khe", probs, grad_out, precision=HIGH)
    grad_p = jnp.einsum("qhe,khe->hqk", grad_out, v, precision=HIGH)
    inner = jnp.sum(grad_out * out, axis=-1)
    grad_s = probs * (grad_p - inner.T[:, :, None]) * factor
    grad_q = jnp.einsum("hqk,khe->qhe", grad_s, k, precision=HIGH)
    grad_k = jnp.einsum("hqk,qhe->khe", grad_s, q, precision=HIGH)
    return (
        grad_q.reshape(queries.shape),
        grad_k.reshape(keys.shape),
        grad_v.reshape(values.shape),
    )


def rows_of(flat, width):
    flat = flat.reshape(-1)
    short = -flat.shape[0] % width
    return jnp.pad(flat, (0, short)).reshape(-1, width)


def pad_rows(rows):
    return jnp.pad(rows, ((0, -rows.shape[0] % 8), (0, 0)))


def attn_pack(weight, out_weight):
    return jnp.concatenate([weight[0], weight[1], weight[2], out_weight.T], axis=1)


def body(
    mel_frames,
    frame_mask,
    token_ids,
    token_mask,
    embedding,
    conv_one,
    conv_two,
    enc_qkv,
    enc_out,
    enc_up,
    enc_down,
    cross_qkv,
    cross_out,
    dec_qkv,
    dec_out,
    dec_up,
    dec_down,
    norm_params,
    cotangent,
):
    n_dp = lax.axis_size("dp")
    dp_place, mp_place = lax.axis_index("dp"), lax.axis_index("mp")
    turned = (mp_place % 2) == 1
    frames = mel_frames.shape[0] // 2
    mel = mel_frames.shape[1]
    tokens, width = cotangent.shape
    local = enc_qkv.shape[2]
    taps, chans = conv_one.shape[0], conv_one.shape[2]

    def turn(rows):
        half = rows.shape[0] // 2
        return jnp.where(turned, jnp.concatenate([rows[half:], rows[:half]], axis=0), rows)

    def positions(count):
        index = lax.broadcasted_iota(jnp.int32, (count, 1), 0)
        return jnp.where(turned, jnp.where(index >= count // 2, index - count // 2, index + count // 2), index)

    def sinusoid(count):
        half_width = width // 2
        rates = jnp.exp(-math.log(10000.0) * jnp.arange(half_width).astype(jnp.float32) / (half_width - 1))
        angles = positions(count).astype(jnp.float32) * rates[None, :]
        return jnp.concatenate([jnp.sin(angles), jnp.cos(angles)], axis=1)

    conv_rows = pad_rows(
        jnp.concatenate(
            [
                conv_two.reshape(-1, width),
                rows_of(conv_one.transpose(2, 0, 1), width),
                rows_of(norm_params, width),
            ],
            axis=0,
        )
    )
    stem_all = gather_data(conv_rows)
    enc_attn_all = gather_slow(attn_pack(enc_qkv, enc_out)).reshape(width, -1)
    dec_attn_all = gather_data(attn_pack(dec_qkv, dec_out)).reshape(width, -1)
    part = width // n_dp
    ff = enc_up.shape[1]
    mlp_cuts = [(0, part, 0, ff), (part, 2 * part, 0, ff)]
    enc_up_all, enc_down_all = split_rows(gather_slow(jnp.concatenate([enc_up, enc_down.T], axis=0)), mlp_cuts)
    cross_all = gather_data(attn_pack(cross_qkv, cross_out)).reshape(width, -1)

    two_rows = taps * chans
    one_size = taps * mel * chans
    one_rows = -(-one_size // width)
    stem_width = n_dp * chans
    w_two = (
        stem_all[:, :two_rows]
        .reshape(n_dp, taps, chans, width)
        .transpose(1, 0, 2, 3)
        .reshape(taps * stem_width, width)
    )
    w_one = (
        stem_all[:, two_rows : two_rows + one_rows]
        .reshape(n_dp, -1)[:, :one_size]
        .reshape(stem_width, taps * mel)
    )
    norms = (
        stem_all[:, two_rows + one_rows :]
        .reshape(n_dp, -1)[:, : 12 * part]
        .reshape(n_dp, 6, 2, part)
        .transpose(1, 2, 0, 3)
        .reshape(6, 2, width)
    )
    w_both = jnp.concatenate(
        [jnp.pad(w_one, ((0, 0), (0, mel))), jnp.pad(w_one, ((0, 0), (mel, 0)))], axis=0
    )

    frame_row = lax.dynamic_index_in_dim(frame_mask, dp_place, 0, keepdims=False) > 0
    token_row = lax.dynamic_index_in_dim(token_mask, dp_place, 0, keepdims=False) > 0
    frame_ok, token_ok = turn(frame_row), turn(token_row)
    frame_allowed = frame_ok[None, :]
    text_at = positions(tokens)
    self_allowed = (text_at.reshape(1, -1) <= text_at) & token_ok[None, :]
    cot = turn(cotangent)

    frame_at = positions(frames)
    first, last = frame_at == 0, frame_at == frames - 1
    both = turn(mel_frames.reshape(frames, 2 * mel))
    before = jnp.where(first, 0.0, jnp.roll(both[:, mel:], 1, axis=0))
    after = jnp.where(last, 0.0, jnp.roll(both[:, :mel], -1, axis=0))
    window = jnp.concatenate([before, both, after], axis=1)
    pre_one = mm_nt(window, w_both)
    stem_one = gelu(pre_one)
    odd = stem_one[:, stem_width:]
    stem_cat = jnp.concatenate([jnp.where(first, 0.0, jnp.roll(odd, 1, axis=0)), stem_one], axis=1)
    stem_part = mm(stem_cat, w_two)
    stem_sum = model_sum(stem_part)
    dec_mlp_shard = tie(jnp.concatenate([dec_up, dec_down.T], axis=0), stem_part)
    dec_up_all, dec_down_all = split_rows(gather_slow(dec_mlp_shard), mlp_cuts)
    stream_zero = gelu(stem_sum) + sinusoid(frames)

    hat_zero, scale_zero = normalize(stream_zero)
    ln_zero = hat_zero * norms[0, 0] + norms[0, 1]
    enc_three = mm(ln_zero, enc_attn_all[:, : 3 * local])
    enc_q, enc_k, enc_v = (enc_three[:, i * local : (i + 1) * local] for i in range(3))
    enc_mixed, enc_lse = attend(enc_q, enc_k, enc_v, frame_allowed)
    enc_attn = model_sum(mm_nt(enc_mixed, enc_attn_all[:, 3 * local :]))
    stream_one = stream_zero + enc_attn
    frame_col = frame_ok.astype(jnp.float32)[:, None]
    token_col = token_ok.astype(jnp.float32)[:, None]
    stream_two, enc_pre, enc_stat = mlp_forward(
        stream_one, norms[1], enc_up_all, enc_down_all, frame_col, 1, "enc_mlp_forward"
    )
    hat_two, scale_two = normalize(stream_two)
    memory = hat_two * norms[2, 0] + norms[2, 1]
    cross_two = mm(memory, cross_all[:, local : 3 * local])
    cross_k, cross_v = cross_two[:, :local], cross_two[:, local:]

    vocab_rows, embed_width = embedding.shape
    local_ids = token_ids.reshape(-1) - dp_place * vocab_rows
    owned = (local_ids >= 0) & (local_ids < vocab_rows)
    safe_ids = jnp.clip(local_ids, 0, vocab_rows - 1)
    picked = jnp.where(owned[:, None], jnp.take(embedding, safe_ids, axis=0), 0.0)
    picked = tie(picked, stem_sum)
    share = lax.psum_scatter(picked, "dp", scatter_dimension=0, tiled=True)
    text_zero = turn(lax.all_gather(share, "mp", axis=1, tiled=True)) + sinusoid(tokens)

    hat_three, scale_three = normalize(text_zero)
    ln_three = hat_three * norms[3, 0] + norms[3, 1]
    dec_three = mm(ln_three, dec_attn_all[:, : 3 * local])
    dec_q, dec_k, dec_v = (dec_three[:, i * local : (i + 1) * local] for i in range(3))
    dec_mixed, dec_lse = attend(dec_q, dec_k, dec_v, self_allowed)
    dec_attn = model_sum(mm_nt(dec_mixed, dec_attn_all[:, 3 * local :]))
    text_one = text_zero + dec_attn
    hat_four, scale_four = normalize(text_one)
    ln_four = hat_four * norms[4, 0] + norms[4, 1]
    cross_q = mm(ln_four, cross_all[:, :local])
    cross_mixed, cross_lse = attend(cross_q, cross_k, cross_v, frame_allowed)
    cross_attn = model_sum(mm_nt(cross_mixed, cross_all[:, 3 * local :]))
    text_two = text_one + cross_attn
    decoded, dec_pre, dec_stat = mlp_forward(
        text_two, norms[5], dec_up_all, dec_down_all, token_col, 2, "dec_mlp_forward"
    )

    def half_of(rows):
        return rows[: rows.shape[0] // 2]

    frame_weight = half_of(frame_ok).astype(jnp.float32)[:, None]
    token_weight = half_of(token_ok).astype(jnp.float32)[:, None]

    def squares(rows, weight):
        kept = half_of(rows)
        return jnp.sum(kept * kept * weight)

    local_sums = jnp.stack(
        [squares(x, frame_weight) for x in (stream_zero, enc_attn)]
        + [jnp.sum(enc_stat[0]), jnp.sum(enc_stat[1])]
        + [squares(x, token_weight) for x in (text_zero, dec_attn, cross_attn)]
        + [jnp.sum(dec_stat[0]), jnp.sum(dec_stat[1])]
    )
    local_sums = local_sums + exchange(local_sums, "mp", 1)
    square_sums = data_sum(local_sums)
    frame_total = jnp.sum((frame_mask > 0).astype(jnp.float32))
    token_total = jnp.sum((token_mask > 0).astype(jnp.float32))
    counts = jnp.concatenate([jnp.full((4,), frame_total), jnp.full((5,), token_total)])
    rms_stats = jnp.sqrt(square_sums / (counts * width))

    def norm_grads(grad, xhat):
        kept = half_of(grad)
        return jnp.stack([jnp.sum(kept * half_of(xhat), axis=0), jnp.sum(kept, axis=0)])

    def block(grad):
        return grad.reshape(n_dp, grad.shape[0] // n_dp, grad.shape[1])

    grad_text_two, grad_up, grad_down, norm_five = mlp_backward(
        cot, text_two, norms[5], dec_pre, dec_up_all, dec_down_all, 3, "dec_mlp_backward"
    )
    grad_dec_up = scatter_slow(block(grad_up))
    grad_dec_down = scatter_slow(block(grad_down))
    norm_five = norm_five[:2]

    grad_cross_out = mm_tn(grad_text_two, cross_mixed)
    grad_cq, grad_ck, grad_cv = attend_back(
        cross_q,
        cross_k,
        cross_v,
        frame_allowed,
        cross_mixed,
        cross_lse,
        mm(grad_text_two, cross_all[:, 3 * local :]),
    )
    grad_ckv = jnp.concatenate([grad_ck, grad_cv], axis=1)
    grad_cross = scatter_slow(
        block(
            jnp.concatenate([mm_tn(ln_four, grad_cq), mm_tn(memory, grad_ckv), grad_cross_out], axis=1)
        )
    )
    grad_memory = model_sum(mm_nt(grad_ckv, cross_all[:, local : 3 * local]))
    grad_ln = model_sum(mm_nt(grad_cq, cross_all[:, :local]))
    norm_four = norm_grads(grad_ln, hat_four)
    grad_text_one = grad_text_two + norm_back(grad_ln, hat_four, scale_four, norms[4, 0])

    grad_dec_out = mm_tn(grad_text_one, dec_mixed)
    grad_three = jnp.concatenate(
        attend_back(
            dec_q,
            dec_k,
            dec_v,
            self_allowed,
            dec_mixed,
            dec_lse,
            mm(grad_text_one, dec_attn_all[:, 3 * local :]),
        ),
        axis=1,
    )
    grad_dec_attn = scatter_slow(
        block(jnp.concatenate([mm_tn(ln_three, grad_three), grad_dec_out], axis=1))
    )
    grad_ln = model_sum(mm_nt(grad_three, dec_attn_all[:, : 3 * local]))
    norm_three = norm_grads(grad_ln, hat_three)
    grad_text_zero = grad_text_one + norm_back(grad_ln, hat_three, scale_three, norms[3, 0])
    grad_share = lax.dynamic_slice_in_dim(turn(grad_text_zero), mp_place * embed_width, embed_width, 1)
    grad_rows = lax.all_gather(grad_share, "dp", axis=0, tiled=True)
    grad_embedding = (
        jnp.zeros(embedding.shape, jnp.float32)
        .at[safe_ids]
        .add(jnp.where(owned[:, None], grad_rows, 0.0))
    )

    norm_two = norm_grads(grad_memory, hat_two)
    grad_stream_two = norm_back(grad_memory, hat_two, scale_two, norms[2, 0])
    grad_stream_one, grad_up, grad_down, norm_one = mlp_backward(
        grad_stream_two, stream_one, norms[1], enc_pre, enc_up_all, enc_down_all, 4, "enc_mlp_backward"
    )
    grad_enc_up = scatter_data(block(grad_up))
    grad_enc_down = scatter_data(block(grad_down))
    norm_one = norm_one[:2]

    grad_enc_out = mm_tn(grad_stream_one, enc_mixed)
    grad_three = jnp.concatenate(
        attend_back(
            enc_q,
            enc_k,
            enc_v,
            frame_allowed,
            enc_mixed,
            enc_lse,
            mm(grad_stream_one, enc_attn_all[:, 3 * local :]),
        ),
        axis=1,
    )
    grad_enc_attn = scatter_data(
        block(jnp.concatenate([mm_tn(ln_zero, grad_three), grad_enc_out], axis=1))
    )
    grad_ln = model_sum(mm_nt(grad_three, enc_attn_all[:, : 3 * local]))
    norm_zero = norm_grads(grad_ln, hat_zero)
    grad_stream_zero = grad_stream_one + norm_back(grad_ln, hat_zero, scale_zero, norms[0, 0])

    grad_stem = grad_stream_zero * gelu_slope(stem_sum)
    grad_w_two = mm_tn(stem_cat, grad_stem)
    grad_cat = mm_nt(grad_stem, w_two)
    grad_back = jnp.roll(jnp.where(first, 0.0, grad_cat[:, :stem_width]), -1, axis=0)
    grad_one = jnp.concatenate(
        [grad_cat[:, stem_width : 2 * stem_width], grad_cat[:, 2 * stem_width :] + grad_back], axis=1
    )
    grad_pre = grad_one * gelu_slope(pre_one)
    grad_both = mm_tn(grad_pre, window)
    grad_w_one = grad_both[:stem_width, : taps * mel] + grad_both[stem_width:, mel:]
    grad_window = mm(grad_pre, w_both)
    grad_mel = grad_window[:, mel : 3 * mel] + jnp.concatenate(
        [
            jnp.roll(jnp.where(last, 0.0, grad_window[:, 3 * mel :]), 1, axis=0),
            jnp.roll(jnp.where(first, 0.0, grad_window[:, :mel]), -1, axis=0),
        ],
        axis=1,
    )
    grad_mel = turn(model_sum(grad_mel)).reshape(mel_frames.shape)

    norm_all = jnp.stack([norm_zero, norm_one, norm_two, norm_three, norm_four, norm_five])
    norm_all = norm_all + exchange(norm_all, "mp", 1)
    norm_blocks = norm_all.reshape(12, n_dp, part).transpose(1, 0, 2).reshape(n_dp, -1)
    one_blocks = grad_w_one.reshape(n_dp, one_size)

    def lay(flat):
        short = -flat.shape[1] % width
        return jnp.pad(flat, ((0, 0), (0, short))).reshape(n_dp, -1, width)

    two_blocks = (
        grad_w_two.reshape(taps, n_dp, chans, width).transpose(1, 0, 2, 3).reshape(n_dp, -1, width)
    )
    stem_blocks = jnp.concatenate([two_blocks, lay(one_blocks), lay(norm_blocks)], axis=1)
    stem_blocks = jnp.pad(stem_blocks, ((0, 0), (0, -stem_blocks.shape[1] % 8), (0, 0)))
    stem_grads = scatter_data(stem_blocks)
    grad_conv_two = stem_grads[:two_rows].reshape(taps, chans, width)
    grad_conv_one = (
        stem_grads[two_rows : two_rows + one_rows]
        .reshape(-1)[:one_size]
        .reshape(chans, taps, mel)
        .transpose(1, 2, 0)
    )
    grad_norms = stem_grads[two_rows + one_rows :].reshape(-1)[: 12 * part].reshape(6, 2, part)

    def three(grads):
        return jnp.stack([grads[:, i * local : (i + 1) * local] for i in range(3)])

    return (
        turn(decoded),
        grad_mel,
        grad_embedding,
        grad_conv_one,
        grad_conv_two,
        three(grad_enc_attn),
        grad_enc_attn[:, 3 * local :].T,
        grad_enc_up,
        grad_enc_down.T,
        three(grad_cross),
        grad_cross[:, 3 * local :].T,
        three(grad_dec_attn),
        grad_dec_attn[:, 3 * local :].T,
        grad_dec_up,
        grad_dec_down.T,
        grad_norms,
        rms_stats,
    )


def solution(mesh):
    placed = (
        P("dp", None),
        P(),
        P(),
        P(),
        P("dp", "mp"),
        P(None, None, ("dp", "mp")),
        P(None, ("dp", "mp"), None),
        P(None, "dp", "mp"),
        P("mp", "dp"),
        P("dp", "mp"),
        P("mp", "dp"),
        P(None, "dp", "mp"),
        P("mp", "dp"),
        P(None, "dp", "mp"),
        P("mp", "dp"),
        P("dp", "mp"),
        P("mp", "dp"),
        P(None, None, "dp"),
        P("dp", None),
    )
    return jax.shard_map(
        body,
        mesh=mesh,
        in_specs=placed,
        out_specs=(
            P("dp", None),
            P("dp", None),
            P("dp", "mp"),
            P(None, None, ("dp", "mp")),
            P(None, ("dp", "mp"), None),
            P(None, "dp", "mp"),
            P("mp", "dp"),
            P("dp", "mp"),
            P("mp", "dp"),
            P(None, "dp", "mp"),
            P("mp", "dp"),
            P(None, "dp", "mp"),
            P("mp", "dp"),
            P("dp", "mp"),
            P("mp", "dp"),
            P(None, None, "dp"),
            P(),
        ),
        check_vma=False,
    )
```

```python
import functools
import math

import jax
import jax.numpy as jnp
from jax import lax
from jax.experimental import pallas as pl
from jax.experimental.pallas import tpu as pltpu
from jax.sharding import PartitionSpec as P

HEAD = 64
HIGH = lax.Precision.HIGH
NEG = -1e30
EPS = 1e-05
RSQRT2 = 1.0 / math.sqrt(2.0)
RSQRT2PI = 1.0 / math.sqrt(2.0 * math.pi)


def dot(left, right, contract):
    return lax.dot_general(
        left, right, (contract, ((), ())), precision=HIGH, preferred_element_type=jnp.float32
    )


def mm(left, right):
    return dot(left, right, ((1,), (0,)))


def mm_nt(left, right):
    return dot(left, right, ((1,), (1,)))


def mm_tn(left, right):
    return dot(left, right, ((0,), (0,)))


def gelu(v):
    return 0.5 * v * (1.0 + lax.erf(v * RSQRT2))


def gelu_slope(v):
    return 0.5 * (1.0 + lax.erf(v * RSQRT2)) + v * (RSQRT2PI * jnp.exp(-0.5 * v * v))


def normalize(rows):
    centre = rows - jnp.mean(rows, axis=-1, keepdims=True)
    scale = lax.rsqrt(jnp.mean(centre * centre, axis=-1, keepdims=True) + EPS)
    return centre * scale, scale


def norm_back(grad, xhat, scale, gain):
    inner = grad * gain
    return (
        inner
        - jnp.mean(inner, axis=-1, keepdims=True)
        - xhat * jnp.mean(inner * xhat, axis=-1, keepdims=True)
    ) * scale


def exchange(value, axis, flip):
    size = lax.axis_size(axis)
    return lax.ppermute(value, axis, [(i, i ^ flip) for i in range(size)])


def model_sum(part):
    if lax.axis_size("mp") != 4:
        raise ValueError("mp size")
    half = part.shape[0] // 2
    pair = part[:half] + exchange(part[half:], "mp", 1)
    total = pair + exchange(pair, "mp", 2)
    return jnp.concatenate([total, exchange(total, "mp", 1)], axis=0)


def place_pieces(pieces):
    count = len(pieces)
    rows, width = pieces[0].shape

    def kernel(*refs):
        out = refs[count]
        place = lax.axis_index("dp")
        for flip in range(count):
            out[jnp.bitwise_xor(place, flip)] = refs[flip][...]

    size = count * rows * width * 4
    return pl.pallas_call(
        kernel,
        out_shape=jax.ShapeDtypeStruct((count, rows, width), jnp.float32),
        in_specs=[pl.BlockSpec(memory_space=pltpu.VMEM)] * count,
        out_specs=pl.BlockSpec(memory_space=pltpu.VMEM),
        cost_estimate=pl.CostEstimate(flops=0, bytes_accessed=2 * size, transcendentals=0),
        name="place_pieces",
    )(*pieces)


def gather_slow(shard):
    return lax.all_gather(shard, "dp", axis=0, tiled=False)


def split_rows(full, cuts):
    out = []
    for r0, r1, c0, c1 in cuts:
        x = full[:, r0:r1, c0:c1].reshape(full.shape[0] * (r1 - r0), c1 - c0)
        hi = lax.reduce_precision(x, 8, 7)
        out.append((hi.astype(BF), (x - hi).astype(BF)))
    return out


def scatter_slow(blocks):
    return lax.psum_scatter(blocks, "dp", scatter_dimension=0, tiled=False)


def together(*values):
    return lax.optimization_barrier(values)


def model_columns(share):
    place = lax.axis_index("mp")
    near = exchange(share, "mp", 1)
    pieces = [share, near, exchange(share, "mp", 2), exchange(near, "mp", 2)]
    rows, width = share.shape
    out = jnp.zeros((rows, len(pieces) * width), share.dtype)
    for flip, piece in enumerate(pieces):
        out = lax.dynamic_update_slice_in_dim(out, piece, (place ^ flip) * width, 1)
    return out


def gather_data(shard):
    count = lax.axis_size("dp")
    if count > 8:
        return lax.all_gather(shard, "dp", axis=0, tiled=False)
    return place_pieces(gather_pieces(shard))


def gather_pieces(shard):
    count = lax.axis_size("dp")
    pieces = [None] * count
    pieces[0] = shard
    for flip in range(2, count, 2):
        pieces[flip] = exchange(shard, "dp", flip)
    for flip in range(0, count, 2):
        pieces[flip + 1] = exchange(pieces[flip], "dp", 1)
    return pieces


def scatter_data(blocks):
    count = lax.axis_size("dp")
    if count > 8:
        return lax.psum_scatter(blocks, "dp", scatter_dimension=0, tiled=False)
    place = lax.axis_index("dp")
    high, low = place // 2, place % 2
    grouped = blocks.reshape((count // 2, 2) + blocks.shape[1:])
    away = lax.dynamic_index_in_dim(grouped, 1 - low, 1, keepdims=False)
    kept = lax.dynamic_index_in_dim(grouped, low, 1, keepdims=False)
    pair = kept + exchange(away, "dp", 1)
    total = lax.dynamic_index_in_dim(pair, high, 0, keepdims=False)
    for flip in range(1, count // 2):
        piece = lax.dynamic_index_in_dim(pair, high ^ flip, 0, keepdims=False)
        total = total + exchange(piece, "dp", 2 * flip)
    return total


def data_sum(value):
    count = lax.axis_size("dp")
    if count > 8:
        return lax.psum(value, "dp")
    flip = 1
    while flip < count:
        value = value + exchange(value, "dp", flip)
        flip *= 2
    return value


MESH = pl.DeviceIdType.MESH
BF = jnp.bfloat16
VMEM_LIMIT = 66_000_000
NN = ((1,), (0,))
NT = ((1,), (1,))
TN = ((0,), (0,))


def split(x):
    hi = x.astype(BF)
    return hi, (x - hi.astype(jnp.float32)).astype(BF)


def bdot(a, b, contract):
    return lax.dot_general(a, b, (contract, ((), ())), preferred_element_type=jnp.float32)


def dot3(a, b, contract):
    return bdot(a[0], b[0], contract) + (bdot(a[0], b[1], contract) + bdot(a[1], b[0], contract))


def take(pair, where):
    return pair[0][where], pair[1][where]


def rows_at(start, count):
    return (pl.ds(start if isinstance(start, int) else pl.multiple_of(start, 8), count), slice(None))


def put(pair, where, value):
    hi, lo = split(value)
    pair[0][where] = hi
    pair[1][where] = lo


def erf(x):
    x = jnp.clip(x, -3.832506856900711, 3.832506856900711)
    s = x * x
    num = s * 0.00022905065861350646 + 0.0034082910107109506
    num = num * s + 0.050955695062380861
    num = num * s + 0.18520832239976145
    num = num * s + 1.128379143519084
    den = s * -1.1791602954361697e-7 + 0.000023547966471313185
    den = den * s + 0.0010179625278914885
    den = den * s + 0.014070470171167667
    den = den * s + 0.11098505178285362
    den = den * s + 0.49746925110067538
    den = den * s + 1.0
    return x * num / den


def k_gelu(v):
    return 0.5 * v * (1.0 + erf(v * RSQRT2))


def k_slope(v):
    return 0.5 * (1.0 + erf(v * RSQRT2)) + v * (RSQRT2PI * jnp.exp(-0.5 * v * v))


class Links:
    def __init__(self, half, tm, bufs, sems):
        self.half, self.tm, self.n = half, tm, half // tm
        self.send_a, self.recv_a, self.send_b, self.recv_b, self.send_c, self.recv_c = bufs
        self.sems = sems
        place = lax.axis_index("mp")
        self.near = place + 1 - 2 * (place % 2)
        self.far = (place + 2) % 4

    def greet(self):
        barrier = pltpu.get_barrier_semaphore()
        for peer in (self.near, self.far):
            pl.semaphore_signal(barrier, inc=1, device_id={"mp": peer}, device_id_type=MESH)
        pl.semaphore_wait(barrier, 2)

    def copy(self, kind, i):
        src, dst, peer = (
            (self.send_a, self.recv_a, self.near),
            (self.send_b, self.recv_b, self.far),
            (self.send_c, self.recv_c, self.near),
        )[kind]
        part = pl.ds(i * self.tm, self.tm)
        return pltpu.make_async_remote_copy(
            src_ref=src.at[part],
            dst_ref=dst.at[part],
            send_sem=self.sems.at[2 * kind, i],
            recv_sem=self.sems.at[2 * kind + 1, i],
            device_id={"mp": peer},
            device_id_type=MESH,
        )

    def begin(self, part_of):
        for i in range(self.n):
            at = rows_at(i * self.tm, self.tm)
            self.send_a[at] = part_of(self.half + i * self.tm)
            self.copy(0, i).start()
            mine = part_of(i * self.tm)
            self.copy(0, i).wait_recv()
            self.send_b[at] = mine + self.recv_a[at]
            self.copy(1, i).start()

    def finish(self, done):
        for i in range(self.n):
            at = rows_at(i * self.tm, self.tm)
            self.copy(1, i).wait_recv()
            total = self.send_b[at] + self.recv_b[at]
            self.send_c[at] = total
            self.copy(2, i).start()
            done(i * self.tm, total, True)
        for i in range(self.n):
            self.copy(2, i).wait_recv()
            done(self.half + i * self.tm, self.recv_c[rows_at(i * self.tm, self.tm)], False)
        for kind in range(3):
            for i in range(self.n):
                self.copy(kind, i).wait_send()


def link_scratch(half, tm, width):
    return [pltpu.VMEM((half, width), jnp.float32)] * 6 + [pltpu.SemaphoreType.DMA((6, half // tm))]


def call(kernel, outs, ins, scratch, name, collective=None, flops=0):
    nbytes = sum(math.prod(x.shape) * x.dtype.itemsize for x in list(ins) + list(outs))
    return pl.pallas_call(
        kernel,
        out_shape=[jax.ShapeDtypeStruct(o.shape, o.dtype) for o in outs],
        in_specs=[pl.BlockSpec(memory_space=pltpu.VMEM)] * len(ins),
        out_specs=[pl.BlockSpec(memory_space=pltpu.VMEM)] * len(outs),
        scratch_shapes=scratch,
        compiler_params=pltpu.CompilerParams(
            vmem_limit_bytes=VMEM_LIMIT,
            collective_id=collective,
            has_side_effects=collective is not None,
        ),
        cost_estimate=pl.CostEstimate(flops=flops, bytes_accessed=nbytes, transcendentals=0),
        name=name,
    )(*ins)


def shape(*dims, dtype=jnp.float32):
    return jax.ShapeDtypeStruct(dims, dtype)


def row_stats(x):
    mean = jnp.mean(x, axis=-1, keepdims=True)
    centre = x - mean
    scale = lax.rsqrt(jnp.mean(centre * centre, axis=-1, keepdims=True) + EPS)
    return centre * scale, scale


def chunk_of(half):
    return 128 if half % 128 == 0 else half


def mlp_forward(x, norm, up, down, weight, collective, name):
    rows, width = x.shape
    ff = up[0].shape[1]
    half = rows // 2
    tm = chunk_of(half)

    def kernel(x_ref, norm_ref, uh, ul, dh, dl, w_ref, out, pre_out, stat, *rest):
        links = Links(half, tm, rest[:6], rest[6])
        links.greet()
        gain, bias = norm_ref[0:1, :], norm_ref[1:2, :]

        def part_of(start):
            at = rows_at(start, tm)
            hat, _ = row_stats(x_ref[at])
            pre = dot3(split(hat * gain + bias), (uh[...], ul[...]), NN)
            pre_out[at] = pre
            return dot3(split(k_gelu(pre)), (dh[...], dl[...]), NT)

        links.begin(part_of)
        stat[...] = jnp.zeros_like(stat)

        def done(start, total, mine):
            at = rows_at(start, tm)
            value = x_ref[at] + total
            out[at] = value
            if mine:
                w = w_ref[at]
                stat[0:1, :] += jnp.sum(total * total * w, axis=0, keepdims=True)
                stat[1:2, :] += jnp.sum(value * value * w, axis=0, keepdims=True)

        links.finish(done)

    return call(
        kernel,
        [shape(rows, width), shape(rows, ff), shape(8, width)],
        [x, norm, *up, *down, weight],
        link_scratch(half, tm, width),
        name,
        collective,
        flops=12 * rows * width * ff,
    )


def mlp_backward(grad, x, norm, pre, up, down, collective, name):
    rows, width = x.shape
    ff = up[0].shape[1]
    half = rows // 2
    tm = chunk_of(half)

    def kernel(g_ref, x_ref, norm_ref, pre_ref, uh, ul, dh, dl, out, dup, ddown, dnorm, lh, ll, ph, plo, hh, hl, gh, gl, *rest):
        links = Links(half, tm, rest[:6], rest[6])
        links.greet()
        gain, bias = norm_ref[0:1, :], norm_ref[1:2, :]

        def part_of(start):
            at = rows_at(start, tm)
            grad_rows = split(g_ref[at])
            gh[at], gl[at] = grad_rows
            pre_rows = pre_ref[at]
            cdf = 0.5 * (1.0 + erf(pre_rows * RSQRT2))
            put((hh, hl), at, pre_rows * cdf)
            slope = cdf + pre_rows * (RSQRT2PI * jnp.exp(-0.5 * pre_rows * pre_rows))
            grad_pre = split(dot3(grad_rows, (dh[...], dl[...]), NN) * slope)
            ph[at], plo[at] = grad_pre
            return dot3(grad_pre, (uh[...], ul[...]), NT)

        links.begin(part_of)

        for start in range(0, rows, tm):
            at = rows_at(start, tm)
            hat, _ = row_stats(x_ref[at])
            put((lh, ll), at, hat * gain + bias)
        step = 256 if width % 256 == 0 else width
        for c in range(0, width, step):
            cols = (slice(None), pl.ds(c, step))
            ddown[pl.ds(c, step), :] = dot3(take((gh, gl), cols), (hh[...], hl[...]), TN)
            dup[pl.ds(c, step), :] = dot3(take((lh, ll), cols), (ph[...], plo[...]), TN)
        dnorm[...] = jnp.zeros_like(dnorm)

        def done(start, total, mine):
            at = rows_at(start, tm)
            hat, scale = row_stats(x_ref[at])
            if mine:
                dnorm[0:1, :] += jnp.sum(total * hat, axis=0, keepdims=True)
                dnorm[1:2, :] += jnp.sum(total, axis=0, keepdims=True)
            out[at] = g_ref[at] + norm_back(total, hat, scale, gain)

        links.finish(done)

    return call(
        kernel,
        [shape(rows, width), shape(width, ff), shape(width, ff), shape(8, width)],
        [grad, x, norm, pre, *up, *down],
        [pltpu.VMEM((rows, width), BF)] * 2
        + [pltpu.VMEM((rows, ff), BF)] * 4
        + [pltpu.VMEM((rows, width), BF)] * 2
        + link_scratch(half, tm, width),
        name,
        collective,
        flops=24 * rows * width * ff,
    )


def split_heads(rows):
    return rows.reshape(rows.shape[0], -1, HEAD)


def attend(queries, keys, values, allowed):
    factor = 1.0 / math.sqrt(HEAD)
    q, k, v = split_heads(queries), split_heads(keys), split_heads(values)
    scores = jnp.einsum("qhe,khe->hqk", q, k, precision=HIGH) * factor
    scores = jnp.where(allowed[None], scores, NEG)
    peaks = jnp.max(scores, axis=-1, keepdims=True)
    weight = jnp.exp(scores - peaks)
    totals = jnp.sum(weight, axis=-1, keepdims=True)
    output = jnp.einsum("hqk,khe->qhe", weight / totals, v, precision=HIGH)
    return output.reshape(queries.shape), peaks + jnp.log(totals)


def attend_back(queries, keys, values, allowed, output, log_total, grad):
    factor = 1.0 / math.sqrt(HEAD)
    q, k, v = split_heads(queries), split_heads(keys), split_heads(values)
    grad_out, out = split_heads(grad), split_heads(output)
    scores = jnp.einsum("qhe,khe->hqk", q, k, precision=HIGH) * factor
    probs = jnp.where(allowed[None], jnp.exp(scores - log_total), 0.0)
    grad_v = jnp.einsum("hqk,qhe->khe", probs, grad_out, precision=HIGH)
    grad_p = jnp.einsum("qhe,khe->hqk", grad_out, v, precision=HIGH)
    inner = jnp.sum(grad_out * out, axis=-1)
    grad_s = probs * (grad_p - inner.T[:, :, None]) * factor
    grad_q = jnp.einsum("hqk,khe->qhe", grad_s, k, precision=HIGH)
    grad_k = jnp.einsum("hqk,qhe->khe", grad_s, q, precision=HIGH)
    return (
        grad_q.reshape(queries.shape),
        grad_k.reshape(keys.shape),
        grad_v.reshape(values.shape),
    )


def rows_of(flat, width):
    flat = flat.reshape(-1)
    short = -flat.shape[0] % width
    return jnp.pad(flat, (0, short)).reshape(-1, width)


def pad_rows(rows):
    return jnp.pad(rows, ((0, -rows.shape[0] % 8), (0, 0)))


def attn_pack(weight, out_weight):
    return jnp.concatenate([weight[0], weight[1], weight[2], out_weight.T], axis=1)


def body(
    mel_frames,
    frame_mask,
    token_ids,
    token_mask,
    embedding,
    conv_one,
    conv_two,
    enc_qkv,
    enc_out,
    enc_up,
    enc_down,
    cross_qkv,
    cross_out,
    dec_qkv,
    dec_out,
    dec_up,
    dec_down,
    norm_params,
    cotangent,
):
    n_dp = lax.axis_size("dp")
    dp_place, mp_place = lax.axis_index("dp"), lax.axis_index("mp")
    turned = (mp_place % 2) == 1
    frames = mel_frames.shape[0] // 2
    mel = mel_frames.shape[1]
    tokens, width = cotangent.shape
    local = enc_qkv.shape[2]
    taps, chans = conv_one.shape[0], conv_one.shape[2]

    def turn(rows):
        half = rows.shape[0] // 2
        return jnp.where(turned, jnp.concatenate([rows[half:], rows[:half]], axis=0), rows)

    def positions(count):
        index = lax.broadcasted_iota(jnp.int32, (count, 1), 0)
        return jnp.where(turned, jnp.where(index >= count // 2, index - count // 2, index + count // 2), index)

    def sinusoid(count):
        half_width = width // 2
        rates = jnp.exp(-math.log(10000.0) * jnp.arange(half_width).astype(jnp.float32) / (half_width - 1))
        angles = positions(count).astype(jnp.float32) * rates[None, :]
        return jnp.concatenate([jnp.sin(angles), jnp.cos(angles)], axis=1)

    conv_rows = pad_rows(
        jnp.concatenate(
            [
                conv_two.reshape(-1, width),
                rows_of(conv_one.transpose(2, 0, 1), width),
                rows_of(norm_params, width),
            ],
            axis=0,
        )
    )
    stem_all = gather_data(conv_rows)
    enc_attn_all = gather_slow(attn_pack(enc_qkv, enc_out)).reshape(width, -1)
    dec_attn_all = gather_data(attn_pack(dec_qkv, dec_out)).reshape(width, -1)
    part = width // n_dp
    ff = enc_up.shape[1]
    mlp_cuts = [(0, part, 0, ff), (part, 2 * part, 0, ff)]
    enc_up_all, enc_down_all = split_rows(gather_slow(jnp.concatenate([enc_up, enc_down.T], axis=0)), mlp_cuts)
    cross_all = gather_data(attn_pack(cross_qkv, cross_out)).reshape(width, -1)

    two_rows = taps * chans
    one_size = taps * mel * chans
    one_rows = -(-one_size // width)
    stem_width = n_dp * chans
    w_two = (
        stem_all[:, :two_rows]
        .reshape(n_dp, taps, chans, width)
        .transpose(1, 0, 2, 3)
        .reshape(taps * stem_width, width)
    )
    w_one = (
        stem_all[:, two_rows : two_rows + one_rows]
        .reshape(n_dp, -1)[:, :one_size]
        .reshape(stem_width, taps * mel)
    )
    norms = (
        stem_all[:, two_rows + one_rows :]
        .reshape(n_dp, -1)[:, : 12 * part]
        .reshape(n_dp, 6, 2, part)
        .transpose(1, 2, 0, 3)
        .reshape(6, 2, width)
    )
    w_both = jnp.concatenate(
        [jnp.pad(w_one, ((0, 0), (0, mel))), jnp.pad(w_one, ((0, 0), (mel, 0)))], axis=0
    )

    frame_row = lax.dynamic_index_in_dim(frame_mask, dp_place, 0, keepdims=False) > 0
    token_row = lax.dynamic_index_in_dim(token_mask, dp_place, 0, keepdims=False) > 0
    frame_ok, token_ok = turn(frame_row), turn(token_row)
    frame_allowed = frame_ok[None, :]
    text_at = positions(tokens)
    self_allowed = (text_at.reshape(1, -1) <= text_at) & token_ok[None, :]
    cot = turn(cotangent)

    vocab_rows, embed_width = embedding.shape
    local_ids = token_ids.reshape(-1) - dp_place * vocab_rows
    owned = (local_ids >= 0) & (local_ids < vocab_rows)
    safe_ids = jnp.clip(local_ids, 0, vocab_rows - 1)
    picked = jnp.where(owned[:, None], jnp.take(embedding, safe_ids, axis=0), 0.0)

    frame_at = positions(frames)
    first, last = frame_at == 0, frame_at == frames - 1
    both = turn(mel_frames.reshape(frames, 2 * mel))
    before = jnp.where(first, 0.0, jnp.roll(both[:, mel:], 1, axis=0))
    after = jnp.where(last, 0.0, jnp.roll(both[:, :mel], -1, axis=0))
    window = jnp.concatenate([before, both, after], axis=1)
    pre_one = mm_nt(window, w_both)
    stem_one = gelu(pre_one)
    odd = stem_one[:, stem_width:]
    stem_cat = jnp.concatenate([jnp.where(first, 0.0, jnp.roll(odd, 1, axis=0)), stem_one], axis=1)
    stem_part, enc_attn_all, picked = together(mm(stem_cat, w_two), enc_attn_all, picked)
    stem_sum = model_sum(stem_part)
    dec_up_all, dec_down_all = split_rows(gather_slow(jnp.concatenate([dec_up, dec_down.T], axis=0)), mlp_cuts)
    stream_zero = gelu(stem_sum) + sinusoid(frames)

    hat_zero, scale_zero = normalize(stream_zero)
    ln_zero = hat_zero * norms[0, 0] + norms[0, 1]
    enc_three = mm(ln_zero, enc_attn_all[:, : 3 * local])
    enc_q, enc_k, enc_v = (enc_three[:, i * local : (i + 1) * local] for i in range(3))
    enc_mixed, enc_lse = attend(enc_q, enc_k, enc_v, frame_allowed)
    enc_attn = model_sum(mm_nt(enc_mixed, enc_attn_all[:, 3 * local :]))
    stream_one = stream_zero + enc_attn
    frame_col = frame_ok.astype(jnp.float32)[:, None]
    token_col = token_ok.astype(jnp.float32)[:, None]
    stream_two, enc_pre, enc_stat = mlp_forward(
        stream_one, norms[1], enc_up_all, enc_down_all, frame_col, 1, "enc_mlp_forward"
    )
    hat_two, scale_two = normalize(stream_two)
    memory = hat_two * norms[2, 0] + norms[2, 1]
    cross_two = mm(memory, cross_all[:, local : 3 * local])
    cross_k, cross_v = cross_two[:, :local], cross_two[:, local:]

    share = lax.psum_scatter(picked, "dp", scatter_dimension=0, tiled=True)
    text_zero = turn(model_columns(share)) + sinusoid(tokens)

    hat_three, scale_three = normalize(text_zero)
    ln_three = hat_three * norms[3, 0] + norms[3, 1]
    dec_three = mm(ln_three, dec_attn_all[:, : 3 * local])
    dec_q, dec_k, dec_v = (dec_three[:, i * local : (i + 1) * local] for i in range(3))
    dec_mixed, dec_lse = attend(dec_q, dec_k, dec_v, self_allowed)
    dec_attn = model_sum(mm_nt(dec_mixed, dec_attn_all[:, 3 * local :]))
    text_one = text_zero + dec_attn
    hat_four, scale_four = normalize(text_one)
    ln_four = hat_four * norms[4, 0] + norms[4, 1]
    cross_q = mm(ln_four, cross_all[:, :local])
    cross_mixed, cross_lse = attend(cross_q, cross_k, cross_v, frame_allowed)
    cross_attn = model_sum(mm_nt(cross_mixed, cross_all[:, 3 * local :]))
    text_two = text_one + cross_attn
    decoded, dec_pre, dec_stat = mlp_forward(
        text_two, norms[5], dec_up_all, dec_down_all, token_col, 2, "dec_mlp_forward"
    )

    def half_of(rows):
        return rows[: rows.shape[0] // 2]

    frame_weight = half_of(frame_ok).astype(jnp.float32)[:, None]
    token_weight = half_of(token_ok).astype(jnp.float32)[:, None]

    def squares(rows, weight):
        kept = half_of(rows)
        return jnp.sum(kept * kept * weight)

    local_sums = jnp.stack(
        [squares(x, frame_weight) for x in (stream_zero, enc_attn)]
        + [jnp.sum(enc_stat[0]), jnp.sum(enc_stat[1])]
        + [squares(x, token_weight) for x in (text_zero, dec_attn, cross_attn)]
        + [jnp.sum(dec_stat[0]), jnp.sum(dec_stat[1])]
    )
    local_sums = local_sums + exchange(local_sums, "mp", 1)
    square_sums = data_sum(local_sums)
    frame_total = jnp.sum((frame_mask > 0).astype(jnp.float32))
    token_total = jnp.sum((token_mask > 0).astype(jnp.float32))
    counts = jnp.concatenate([jnp.full((4,), frame_total), jnp.full((5,), token_total)])
    rms_stats = jnp.sqrt(square_sums / (counts * width))

    def norm_grads(grad, xhat):
        kept = half_of(grad)
        return jnp.stack([jnp.sum(kept * half_of(xhat), axis=0), jnp.sum(kept, axis=0)])

    def block(grad):
        return grad.reshape(n_dp, grad.shape[0] // n_dp, grad.shape[1])

    grad_text_two, grad_up, grad_down, norm_five = mlp_backward(
        cot, text_two, norms[5], dec_pre, dec_up_all, dec_down_all, 3, "dec_mlp_backward"
    )
    grad_dec_up = scatter_slow(block(grad_up))
    grad_dec_down = scatter_slow(block(grad_down))
    norm_five = norm_five[:2]

    grad_cross_out = mm_tn(grad_text_two, cross_mixed)
    grad_cq, grad_ck, grad_cv = attend_back(
        cross_q,
        cross_k,
        cross_v,
        frame_allowed,
        cross_mixed,
        cross_lse,
        mm(grad_text_two, cross_all[:, 3 * local :]),
    )
    grad_ckv = jnp.concatenate([grad_ck, grad_cv], axis=1)
    grad_cross = scatter_slow(
        block(
            jnp.concatenate([mm_tn(ln_four, grad_cq), mm_tn(memory, grad_ckv), grad_cross_out], axis=1)
        )
    )
    grad_memory = model_sum(mm_nt(grad_ckv, cross_all[:, local : 3 * local]))
    grad_ln = model_sum(mm_nt(grad_cq, cross_all[:, :local]))
    norm_four = norm_grads(grad_ln, hat_four)
    grad_text_one = grad_text_two + norm_back(grad_ln, hat_four, scale_four, norms[4, 0])

    grad_dec_out = mm_tn(grad_text_one, dec_mixed)
    grad_three = jnp.concatenate(
        attend_back(
            dec_q,
            dec_k,
            dec_v,
            self_allowed,
            dec_mixed,
            dec_lse,
            mm(grad_text_one, dec_attn_all[:, 3 * local :]),
        ),
        axis=1,
    )
    grad_dec_attn = scatter_slow(
        block(jnp.concatenate([mm_tn(ln_three, grad_three), grad_dec_out], axis=1))
    )
    grad_ln = model_sum(mm_nt(grad_three, dec_attn_all[:, : 3 * local]))
    norm_three = norm_grads(grad_ln, hat_three)
    grad_text_zero = grad_text_one + norm_back(grad_ln, hat_three, scale_three, norms[3, 0])
    grad_share = lax.dynamic_slice_in_dim(turn(grad_text_zero), mp_place * embed_width, embed_width, 1)
    grad_rows = lax.all_gather(grad_share, "dp", axis=0, tiled=True)
    grad_embedding = (
        jnp.zeros(embedding.shape, jnp.float32)
        .at[safe_ids]
        .add(jnp.where(owned[:, None], grad_rows, 0.0))
    )

    norm_two = norm_grads(grad_memory, hat_two)
    grad_stream_two = norm_back(grad_memory, hat_two, scale_two, norms[2, 0])
    grad_stream_one, grad_up, grad_down, norm_one = mlp_backward(
        grad_stream_two, stream_one, norms[1], enc_pre, enc_up_all, enc_down_all, 4, "enc_mlp_backward"
    )
    grad_enc_up = scatter_data(block(grad_up))
    grad_enc_down = scatter_data(block(grad_down))
    norm_one = norm_one[:2]

    grad_enc_out = mm_tn(grad_stream_one, enc_mixed)
    grad_three = jnp.concatenate(
        attend_back(
            enc_q,
            enc_k,
            enc_v,
            frame_allowed,
            enc_mixed,
            enc_lse,
            mm(grad_stream_one, enc_attn_all[:, 3 * local :]),
        ),
        axis=1,
    )
    grad_enc_attn = scatter_data(
        block(jnp.concatenate([mm_tn(ln_zero, grad_three), grad_enc_out], axis=1))
    )
    grad_ln = model_sum(mm_nt(grad_three, enc_attn_all[:, : 3 * local]))
    norm_zero = norm_grads(grad_ln, hat_zero)
    grad_stream_zero = grad_stream_one + norm_back(grad_ln, hat_zero, scale_zero, norms[0, 0])

    grad_stem = grad_stream_zero * gelu_slope(stem_sum)
    grad_w_two = mm_tn(stem_cat, grad_stem)
    grad_cat = mm_nt(grad_stem, w_two)
    grad_back = jnp.roll(jnp.where(first, 0.0, grad_cat[:, :stem_width]), -1, axis=0)
    grad_one = jnp.concatenate(
        [grad_cat[:, stem_width : 2 * stem_width], grad_cat[:, 2 * stem_width :] + grad_back], axis=1
    )
    grad_pre = grad_one * gelu_slope(pre_one)
    grad_both = mm_tn(grad_pre, window)
    grad_w_one = grad_both[:stem_width, : taps * mel] + grad_both[stem_width:, mel:]
    grad_window = mm(grad_pre, w_both)
    grad_mel = grad_window[:, mel : 3 * mel] + jnp.concatenate(
        [
            jnp.roll(jnp.where(last, 0.0, grad_window[:, 3 * mel :]), 1, axis=0),
            jnp.roll(jnp.where(first, 0.0, grad_window[:, :mel]), -1, axis=0),
        ],
        axis=1,
    )
    grad_mel = turn(model_sum(grad_mel)).reshape(mel_frames.shape)

    norm_all = jnp.stack([norm_zero, norm_one, norm_two, norm_three, norm_four, norm_five])
    norm_all = norm_all + exchange(norm_all, "mp", 1)
    norm_blocks = norm_all.reshape(12, n_dp, part).transpose(1, 0, 2).reshape(n_dp, -1)
    one_blocks = grad_w_one.reshape(n_dp, one_size)

    def lay(flat):
        short = -flat.shape[1] % width
        return jnp.pad(flat, ((0, 0), (0, short))).reshape(n_dp, -1, width)

    two_blocks = (
        grad_w_two.reshape(taps, n_dp, chans, width).transpose(1, 0, 2, 3).reshape(n_dp, -1, width)
    )
    stem_blocks = jnp.concatenate([two_blocks, lay(one_blocks), lay(norm_blocks)], axis=1)
    stem_blocks = jnp.pad(stem_blocks, ((0, 0), (0, -stem_blocks.shape[1] % 8), (0, 0)))
    stem_grads = scatter_data(stem_blocks)
    grad_conv_two = stem_grads[:two_rows].reshape(taps, chans, width)
    grad_conv_one = (
        stem_grads[two_rows : two_rows + one_rows]
        .reshape(-1)[:one_size]
        .reshape(chans, taps, mel)
        .transpose(1, 2, 0)
    )
    grad_norms = stem_grads[two_rows + one_rows :].reshape(-1)[: 12 * part].reshape(6, 2, part)

    def three(grads):
        return jnp.stack([grads[:, i * local : (i + 1) * local] for i in range(3)])

    return (
        turn(decoded),
        grad_mel,
        grad_embedding,
        grad_conv_one,
        grad_conv_two,
        three(grad_enc_attn),
        grad_enc_attn[:, 3 * local :].T,
        grad_enc_up,
        grad_enc_down.T,
        three(grad_cross),
        grad_cross[:, 3 * local :].T,
        three(grad_dec_attn),
        grad_dec_attn[:, 3 * local :].T,
        grad_dec_up,
        grad_dec_down.T,
        grad_norms,
        rms_stats,
    )


def solution(mesh):
    placed = (
        P("dp", None),
        P(),
        P(),
        P(),
        P("dp", "mp"),
        P(None, None, ("dp", "mp")),
        P(None, ("dp", "mp"), None),
        P(None, "dp", "mp"),
        P("mp", "dp"),
        P("dp", "mp"),
        P("mp", "dp"),
        P(None, "dp", "mp"),
        P("mp", "dp"),
        P(None, "dp", "mp"),
        P("mp", "dp"),
        P("dp", "mp"),
        P("mp", "dp"),
        P(None, None, "dp"),
        P("dp", None),
    )
    return jax.shard_map(
        body,
        mesh=mesh,
        in_specs=placed,
        out_specs=(
            P("dp", None),
            P("dp", None),
            P("dp", "mp"),
            P(None, None, ("dp", "mp")),
            P(None, ("dp", "mp"), None),
            P(None, "dp", "mp"),
            P("mp", "dp"),
            P("dp", "mp"),
            P("mp", "dp"),
            P(None, "dp", "mp"),
            P("mp", "dp"),
            P(None, "dp", "mp"),
            P("mp", "dp"),
            P("dp", "mp"),
            P("mp", "dp"),
            P(None, None, "dp"),
            P(),
        ),
        check_vma=False,
    )
```

```python
import functools
import math

import jax
import jax.numpy as jnp
from jax import lax
from jax.experimental import pallas as pl
from jax.experimental.pallas import tpu as pltpu
from jax.sharding import PartitionSpec as P

HEAD = 64
HIGH = lax.Precision.HIGH
NEG = -1e30
EPS = 1e-05
RSQRT2 = 1.0 / math.sqrt(2.0)
RSQRT2PI = 1.0 / math.sqrt(2.0 * math.pi)


def dot(left, right, contract):
    return lax.dot_general(
        left, right, (contract, ((), ())), precision=HIGH, preferred_element_type=jnp.float32
    )


def mm(left, right):
    return dot(left, right, ((1,), (0,)))


def mm_nt(left, right):
    return dot(left, right, ((1,), (1,)))


def mm_tn(left, right):
    return dot(left, right, ((0,), (0,)))


def gelu(v):
    return 0.5 * v * (1.0 + lax.erf(v * RSQRT2))


def gelu_slope(v):
    return 0.5 * (1.0 + lax.erf(v * RSQRT2)) + v * (RSQRT2PI * jnp.exp(-0.5 * v * v))


def normalize(rows):
    centre = rows - jnp.mean(rows, axis=-1, keepdims=True)
    scale = lax.rsqrt(jnp.mean(centre * centre, axis=-1, keepdims=True) + EPS)
    return centre * scale, scale


def norm_back(grad, xhat, scale, gain):
    inner = grad * gain
    return (
        inner
        - jnp.mean(inner, axis=-1, keepdims=True)
        - xhat * jnp.mean(inner * xhat, axis=-1, keepdims=True)
    ) * scale


def exchange(value, axis, flip):
    size = lax.axis_size(axis)
    return lax.ppermute(value, axis, [(i, i ^ flip) for i in range(size)])


def model_sum(part):
    if lax.axis_size("mp") != 4:
        raise ValueError("mp size")
    half = part.shape[0] // 2
    pair = part[:half] + exchange(part[half:], "mp", 1)
    total = pair + exchange(pair, "mp", 2)
    return jnp.concatenate([total, exchange(total, "mp", 1)], axis=0)


def place_pieces(pieces):
    count = len(pieces)
    rows, width = pieces[0].shape

    def kernel(*refs):
        out = refs[count]
        place = lax.axis_index("dp")
        for flip in range(count):
            out[jnp.bitwise_xor(place, flip)] = refs[flip][...]

    size = count * rows * width * 4
    return pl.pallas_call(
        kernel,
        out_shape=jax.ShapeDtypeStruct((count, rows, width), jnp.float32),
        in_specs=[pl.BlockSpec(memory_space=pltpu.VMEM)] * count,
        out_specs=pl.BlockSpec(memory_space=pltpu.VMEM),
        cost_estimate=pl.CostEstimate(flops=0, bytes_accessed=2 * size, transcendentals=0),
        name="place_pieces",
    )(*pieces)


def gather_slow(shard):
    return lax.all_gather(shard, "dp", axis=0, tiled=False)


def split_rows(full, cuts):
    out = []
    for r0, r1, c0, c1 in cuts:
        x = full[:, r0:r1, c0:c1].reshape(full.shape[0] * (r1 - r0), c1 - c0)
        hi = lax.reduce_precision(x, 8, 7)
        out.append((hi.astype(BF), (x - hi).astype(BF)))
    return out


def scatter_slow(blocks):
    return lax.psum_scatter(blocks, "dp", scatter_dimension=0, tiled=False)


def together(*values):
    return lax.optimization_barrier(values)


def model_columns(share):
    place = lax.axis_index("mp")
    near = exchange(share, "mp", 1)
    pieces = [share, near, exchange(share, "mp", 2), exchange(near, "mp", 2)]
    rows, width = share.shape
    out = jnp.zeros((rows, len(pieces) * width), share.dtype)
    for flip, piece in enumerate(pieces):
        out = lax.dynamic_update_slice_in_dim(out, piece, (place ^ flip) * width, 1)
    return out


def gather_data(shard):
    count = lax.axis_size("dp")
    if count > 8:
        return lax.all_gather(shard, "dp", axis=0, tiled=False)
    return place_pieces(gather_pieces(shard))


def gather_pieces(shard):
    count = lax.axis_size("dp")
    pieces = [None] * count
    pieces[0] = shard
    for flip in range(2, count, 2):
        pieces[flip] = exchange(shard, "dp", flip)
    for flip in range(0, count, 2):
        pieces[flip + 1] = exchange(pieces[flip], "dp", 1)
    return pieces


def scatter_data(blocks):
    count = lax.axis_size("dp")
    if count > 8:
        return lax.psum_scatter(blocks, "dp", scatter_dimension=0, tiled=False)
    place = lax.axis_index("dp")
    high, low = place // 2, place % 2
    grouped = blocks.reshape((count // 2, 2) + blocks.shape[1:])
    away = lax.dynamic_index_in_dim(grouped, 1 - low, 1, keepdims=False)
    kept = lax.dynamic_index_in_dim(grouped, low, 1, keepdims=False)
    pair = kept + exchange(away, "dp", 1)
    total = lax.dynamic_index_in_dim(pair, high, 0, keepdims=False)
    for flip in range(1, count // 2):
        piece = lax.dynamic_index_in_dim(pair, high ^ flip, 0, keepdims=False)
        total = total + exchange(piece, "dp", 2 * flip)
    return total


def data_sum(value):
    count = lax.axis_size("dp")
    if count > 8:
        return lax.psum(value, "dp")
    flip = 1
    while flip < count:
        value = value + exchange(value, "dp", flip)
        flip *= 2
    return value


MESH = pl.DeviceIdType.MESH
BF = jnp.bfloat16
VMEM_LIMIT = 66_000_000
NN = ((1,), (0,))
NT = ((1,), (1,))
TN = ((0,), (0,))


def split(x):
    hi = x.astype(BF)
    return hi, (x - hi.astype(jnp.float32)).astype(BF)


def bdot(a, b, contract):
    return lax.dot_general(a, b, (contract, ((), ())), preferred_element_type=jnp.float32)


def dot3(a, b, contract):
    return bdot(a[0], b[0], contract) + (bdot(a[0], b[1], contract) + bdot(a[1], b[0], contract))


def take(pair, where):
    return pair[0][where], pair[1][where]


def rows_at(start, count):
    return (pl.ds(start if isinstance(start, int) else pl.multiple_of(start, 8), count), slice(None))


def put(pair, where, value):
    hi, lo = split(value)
    pair[0][where] = hi
    pair[1][where] = lo


def erf(x):
    x = jnp.clip(x, -3.832506856900711, 3.832506856900711)
    s = x * x
    num = s * 0.00022905065861350646 + 0.0034082910107109506
    num = num * s + 0.050955695062380861
    num = num * s + 0.18520832239976145
    num = num * s + 1.128379143519084
    den = s * -1.1791602954361697e-7 + 0.000023547966471313185
    den = den * s + 0.0010179625278914885
    den = den * s + 0.014070470171167667
    den = den * s + 0.11098505178285362
    den = den * s + 0.49746925110067538
    den = den * s + 1.0
    return x * num / den


def k_gelu(v):
    return 0.5 * v * (1.0 + erf(v * RSQRT2))


def k_slope(v):
    return 0.5 * (1.0 + erf(v * RSQRT2)) + v * (RSQRT2PI * jnp.exp(-0.5 * v * v))


class Links:
    def __init__(self, half, tm, bufs, sems):
        self.half, self.tm, self.n = half, tm, half // tm
        self.send_a, self.recv_a, self.send_b, self.recv_b, self.send_c, self.recv_c = bufs
        self.sems = sems
        place = lax.axis_index("mp")
        self.near = place + 1 - 2 * (place % 2)
        self.far = (place + 2) % 4

    def greet(self):
        barrier = pltpu.get_barrier_semaphore()
        for peer in (self.near, self.far):
            pl.semaphore_signal(barrier, inc=1, device_id={"mp": peer}, device_id_type=MESH)
        pl.semaphore_wait(barrier, 2)

    def copy(self, kind, i):
        src, dst, peer = (
            (self.send_a, self.recv_a, self.near),
            (self.send_b, self.recv_b, self.far),
            (self.send_c, self.recv_c, self.near),
        )[kind]
        part = pl.ds(i * self.tm, self.tm)
        return pltpu.make_async_remote_copy(
            src_ref=src.at[part],
            dst_ref=dst.at[part],
            send_sem=self.sems.at[2 * kind, i],
            recv_sem=self.sems.at[2 * kind + 1, i],
            device_id={"mp": peer},
            device_id_type=MESH,
        )

    def begin(self, part_of):
        for i in range(self.n):
            at = rows_at(i * self.tm, self.tm)
            self.send_a[at] = part_of(self.half + i * self.tm)
            self.copy(0, i).start()
            mine = part_of(i * self.tm)
            self.copy(0, i).wait_recv()
            self.send_b[at] = mine + self.recv_a[at]
            self.copy(1, i).start()

    def finish(self, done):
        for i in range(self.n):
            at = rows_at(i * self.tm, self.tm)
            self.copy(1, i).wait_recv()
            total = self.send_b[at] + self.recv_b[at]
            self.send_c[at] = total
            self.copy(2, i).start()
            done(i * self.tm, total, True)
        for i in range(self.n):
            self.copy(2, i).wait_recv()
            done(self.half + i * self.tm, self.recv_c[rows_at(i * self.tm, self.tm)], False)
        for kind in range(3):
            for i in range(self.n):
                self.copy(kind, i).wait_send()


def link_scratch(half, tm, width):
    return [pltpu.VMEM((half, width), jnp.float32)] * 6 + [pltpu.SemaphoreType.DMA((6, half // tm))]


def call(kernel, outs, ins, scratch, name, collective=None, flops=0):
    nbytes = sum(math.prod(x.shape) * x.dtype.itemsize for x in list(ins) + list(outs))
    return pl.pallas_call(
        kernel,
        out_shape=[jax.ShapeDtypeStruct(o.shape, o.dtype) for o in outs],
        in_specs=[pl.BlockSpec(memory_space=pltpu.VMEM)] * len(ins),
        out_specs=[pl.BlockSpec(memory_space=pltpu.VMEM)] * len(outs),
        scratch_shapes=scratch,
        compiler_params=pltpu.CompilerParams(
            vmem_limit_bytes=VMEM_LIMIT,
            collective_id=collective,
            has_side_effects=collective is not None,
        ),
        cost_estimate=pl.CostEstimate(flops=flops, bytes_accessed=nbytes, transcendentals=0),
        name=name,
    )(*ins)


def shape(*dims, dtype=jnp.float32):
    return jax.ShapeDtypeStruct(dims, dtype)


def row_stats(x):
    mean = jnp.mean(x, axis=-1, keepdims=True)
    centre = x - mean
    scale = lax.rsqrt(jnp.mean(centre * centre, axis=-1, keepdims=True) + EPS)
    return centre * scale, scale


def chunk_of(half):
    return 128 if half % 128 == 0 else half


def mlp_forward(x, norm, up, down, weight, collective, name):
    rows, width = x.shape
    ff = up[0].shape[1]
    half = rows // 2
    tm = chunk_of(half)

    def kernel(x_ref, norm_ref, uh, ul, dh, dl, w_ref, out, pre_out, stat, *rest):
        links = Links(half, tm, rest[:6], rest[6])
        links.greet()
        gain, bias = norm_ref[0:1, :], norm_ref[1:2, :]

        def part_of(start):
            at = rows_at(start, tm)
            hat, _ = row_stats(x_ref[at])
            pre = dot3(split(hat * gain + bias), (uh[...], ul[...]), NN)
            pre_out[at] = pre
            return dot3(split(k_gelu(pre)), (dh[...], dl[...]), NT)

        links.begin(part_of)
        stat[...] = jnp.zeros_like(stat)

        def done(start, total, mine):
            at = rows_at(start, tm)
            value = x_ref[at] + total
            out[at] = value
            if mine:
                w = w_ref[at]
                stat[0:1, :] += jnp.sum(total * total * w, axis=0, keepdims=True)
                stat[1:2, :] += jnp.sum(value * value * w, axis=0, keepdims=True)

        links.finish(done)

    return call(
        kernel,
        [shape(rows, width), shape(rows, ff), shape(8, width)],
        [x, norm, *up, *down, weight],
        link_scratch(half, tm, width),
        name,
        collective,
        flops=12 * rows * width * ff,
    )


def mlp_backward(grad, x, norm, pre, up, down, collective, name):
    rows, width = x.shape
    ff = up[0].shape[1]
    half = rows // 2
    tm = chunk_of(half)

    def kernel(g_ref, x_ref, norm_ref, pre_ref, uh, ul, dh, dl, out, dup, ddown, dnorm, lh, ll, ph, plo, hh, hl, gh, gl, *rest):
        links = Links(half, tm, rest[:6], rest[6])
        links.greet()
        gain, bias = norm_ref[0:1, :], norm_ref[1:2, :]

        def part_of(start):
            at = rows_at(start, tm)
            grad_rows = split(g_ref[at])
            gh[at], gl[at] = grad_rows
            pre_rows = pre_ref[at]
            cdf = 0.5 * (1.0 + erf(pre_rows * RSQRT2))
            put((hh, hl), at, pre_rows * cdf)
            slope = cdf + pre_rows * (RSQRT2PI * jnp.exp(-0.5 * pre_rows * pre_rows))
            grad_pre = split(dot3(grad_rows, (dh[...], dl[...]), NN) * slope)
            ph[at], plo[at] = grad_pre
            return dot3(grad_pre, (uh[...], ul[...]), NT)

        links.begin(part_of)

        for start in range(0, rows, tm):
            at = rows_at(start, tm)
            hat, _ = row_stats(x_ref[at])
            put((lh, ll), at, hat * gain + bias)
        step = 256 if width % 256 == 0 else width
        for c in range(0, width, step):
            cols = (slice(None), pl.ds(c, step))
            ddown[pl.ds(c, step), :] = dot3(take((gh, gl), cols), (hh[...], hl[...]), TN)
            dup[pl.ds(c, step), :] = dot3(take((lh, ll), cols), (ph[...], plo[...]), TN)
        dnorm[...] = jnp.zeros_like(dnorm)

        def done(start, total, mine):
            at = rows_at(start, tm)
            hat, scale = row_stats(x_ref[at])
            if mine:
                dnorm[0:1, :] += jnp.sum(total * hat, axis=0, keepdims=True)
                dnorm[1:2, :] += jnp.sum(total, axis=0, keepdims=True)
            out[at] = g_ref[at] + norm_back(total, hat, scale, gain)

        links.finish(done)

    return call(
        kernel,
        [shape(rows, width), shape(width, ff), shape(width, ff), shape(8, width)],
        [grad, x, norm, pre, *up, *down],
        [pltpu.VMEM((rows, width), BF)] * 2
        + [pltpu.VMEM((rows, ff), BF)] * 4
        + [pltpu.VMEM((rows, width), BF)] * 2
        + link_scratch(half, tm, width),
        name,
        collective,
        flops=24 * rows * width * ff,
    )


def split_heads(rows):
    return rows.reshape(rows.shape[0], -1, HEAD)


def attend(queries, keys, values, allowed):
    factor = 1.0 / math.sqrt(HEAD)
    q, k, v = split_heads(queries), split_heads(keys), split_heads(values)
    scores = jnp.einsum("qhe,khe->hqk", q, k, precision=HIGH) * factor
    scores = jnp.where(allowed[None], scores, NEG)
    peaks = jnp.max(scores, axis=-1, keepdims=True)
    weight = jnp.exp(scores - peaks)
    totals = jnp.sum(weight, axis=-1, keepdims=True)
    output = jnp.einsum("hqk,khe->qhe", weight / totals, v, precision=HIGH)
    return output.reshape(queries.shape), peaks + jnp.log(totals)


def attend_back(queries, keys, values, allowed, output, log_total, grad):
    factor = 1.0 / math.sqrt(HEAD)
    q, k, v = split_heads(queries), split_heads(keys), split_heads(values)
    grad_out, out = split_heads(grad), split_heads(output)
    scores = jnp.einsum("qhe,khe->hqk", q, k, precision=HIGH) * factor
    probs = jnp.where(allowed[None], jnp.exp(scores - log_total), 0.0)
    grad_v = jnp.einsum("hqk,qhe->khe", probs, grad_out, precision=HIGH)
    grad_p = jnp.einsum("qhe,khe->hqk", grad_out, v, precision=HIGH)
    inner = jnp.sum(grad_out * out, axis=-1)
    grad_s = probs * (grad_p - inner.T[:, :, None]) * factor
    grad_q = jnp.einsum("hqk,khe->qhe", grad_s, k, precision=HIGH)
    grad_k = jnp.einsum("hqk,qhe->khe", grad_s, q, precision=HIGH)
    return (
        grad_q.reshape(queries.shape),
        grad_k.reshape(keys.shape),
        grad_v.reshape(values.shape),
    )


def rows_of(flat, width):
    flat = flat.reshape(-1)
    short = -flat.shape[0] % width
    return jnp.pad(flat, (0, short)).reshape(-1, width)


def pad_rows(rows):
    return jnp.pad(rows, ((0, -rows.shape[0] % 8), (0, 0)))


def attn_pack(weight, out_weight):
    return jnp.concatenate([weight[0], weight[1], weight[2], out_weight.T], axis=1)


def body(
    mel_frames,
    frame_mask,
    token_ids,
    token_mask,
    embedding,
    conv_one,
    conv_two,
    enc_qkv,
    enc_out,
    enc_up,
    enc_down,
    cross_qkv,
    cross_out,
    dec_qkv,
    dec_out,
    dec_up,
    dec_down,
    norm_params,
    cotangent,
):
    n_dp = lax.axis_size("dp")
    dp_place, mp_place = lax.axis_index("dp"), lax.axis_index("mp")
    turned = (mp_place % 2) == 1
    frames = mel_frames.shape[0] // 2
    mel = mel_frames.shape[1]
    tokens, width = cotangent.shape
    local = enc_qkv.shape[2]
    taps, chans = conv_one.shape[0], conv_one.shape[2]

    def turn(rows):
        half = rows.shape[0] // 2
        return jnp.where(turned, jnp.concatenate([rows[half:], rows[:half]], axis=0), rows)

    def positions(count):
        index = lax.broadcasted_iota(jnp.int32, (count, 1), 0)
        return jnp.where(turned, jnp.where(index >= count // 2, index - count // 2, index + count // 2), index)

    def sinusoid(count):
        half_width = width // 2
        rates = jnp.exp(-math.log(10000.0) * jnp.arange(half_width).astype(jnp.float32) / (half_width - 1))
        angles = positions(count).astype(jnp.float32) * rates[None, :]
        return jnp.concatenate([jnp.sin(angles), jnp.cos(angles)], axis=1)

    conv_rows = pad_rows(
        jnp.concatenate(
            [
                conv_two.reshape(-1, width),
                rows_of(conv_one.transpose(2, 0, 1), width),
                rows_of(norm_params, width),
            ],
            axis=0,
        )
    )
    stem_all = gather_data(conv_rows)
    enc_attn_all = gather_slow(attn_pack(enc_qkv, enc_out)).reshape(width, -1)
    dec_attn_all = gather_data(attn_pack(dec_qkv, dec_out)).reshape(width, -1)
    part = width // n_dp
    ff = enc_up.shape[1]
    mlp_cuts = [(0, part, 0, ff), (part, 2 * part, 0, ff)]
    enc_up_all, enc_down_all = split_rows(gather_slow(jnp.concatenate([enc_up, enc_down.T], axis=0)), mlp_cuts)
    cross_all = gather_data(attn_pack(cross_qkv, cross_out)).reshape(width, -1)

    two_rows = taps * chans
    one_size = taps * mel * chans
    one_rows = -(-one_size // width)
    stem_width = n_dp * chans
    w_two = (
        stem_all[:, :two_rows]
        .reshape(n_dp, taps, chans, width)
        .transpose(1, 0, 2, 3)
        .reshape(taps * stem_width, width)
    )
    w_one = (
        stem_all[:, two_rows : two_rows + one_rows]
        .reshape(n_dp, -1)[:, :one_size]
        .reshape(stem_width, taps * mel)
    )
    norms = (
        stem_all[:, two_rows + one_rows :]
        .reshape(n_dp, -1)[:, : 12 * part]
        .reshape(n_dp, 6, 2, part)
        .transpose(1, 2, 0, 3)
        .reshape(6, 2, width)
    )
    w_both = jnp.concatenate(
        [jnp.pad(w_one, ((0, 0), (0, mel))), jnp.pad(w_one, ((0, 0), (mel, 0)))], axis=0
    )

    frame_row = lax.dynamic_index_in_dim(frame_mask, dp_place, 0, keepdims=False) > 0
    token_row = lax.dynamic_index_in_dim(token_mask, dp_place, 0, keepdims=False) > 0
    frame_ok, token_ok = turn(frame_row), turn(token_row)
    frame_allowed = frame_ok[None, :]
    text_at = positions(tokens)
    self_allowed = (text_at.reshape(1, -1) <= text_at) & token_ok[None, :]
    cot = turn(cotangent)

    vocab_rows, embed_width = embedding.shape
    local_ids = token_ids.reshape(-1) - dp_place * vocab_rows
    owned = (local_ids >= 0) & (local_ids < vocab_rows)
    safe_ids = jnp.clip(local_ids, 0, vocab_rows - 1)
    picked = jnp.where(owned[:, None], jnp.take(embedding, safe_ids, axis=0), 0.0)

    frame_at = positions(frames)
    first, last = frame_at == 0, frame_at == frames - 1
    both = turn(mel_frames.reshape(frames, 2 * mel))
    before = jnp.where(first, 0.0, jnp.roll(both[:, mel:], 1, axis=0))
    after = jnp.where(last, 0.0, jnp.roll(both[:, :mel], -1, axis=0))
    window = jnp.concatenate([before, both, after], axis=1)
    pre_one = mm_nt(window, w_both)
    stem_one = gelu(pre_one)
    odd = stem_one[:, stem_width:]
    stem_cat = jnp.concatenate([jnp.where(first, 0.0, jnp.roll(odd, 1, axis=0)), stem_one], axis=1)
    stem_part, enc_attn_all, picked = together(mm(stem_cat, w_two), enc_attn_all, picked)
    stem_sum = model_sum(stem_part)
    dec_up_all, dec_down_all = split_rows(gather_slow(jnp.concatenate([dec_up, dec_down.T], axis=0)), mlp_cuts)
    stream_zero = gelu(stem_sum) + sinusoid(frames)

    hat_zero, scale_zero = normalize(stream_zero)
    ln_zero = hat_zero * norms[0, 0] + norms[0, 1]
    enc_three = mm(ln_zero, enc_attn_all[:, : 3 * local])
    enc_q, enc_k, enc_v = (enc_three[:, i * local : (i + 1) * local] for i in range(3))
    enc_mixed, enc_lse = attend(enc_q, enc_k, enc_v, frame_allowed)
    enc_attn = model_sum(mm_nt(enc_mixed, enc_attn_all[:, 3 * local :]))
    stream_one = stream_zero + enc_attn
    frame_col = frame_ok.astype(jnp.float32)[:, None]
    token_col = token_ok.astype(jnp.float32)[:, None]
    stream_two, enc_pre, enc_stat = mlp_forward(
        stream_one, norms[1], enc_up_all, enc_down_all, frame_col, 1, "enc_mlp_forward"
    )
    hat_two, scale_two = normalize(stream_two)
    memory = hat_two * norms[2, 0] + norms[2, 1]
    cross_two = mm(memory, cross_all[:, local : 3 * local])
    cross_k, cross_v = cross_two[:, :local], cross_two[:, local:]

    share = lax.psum_scatter(picked, "dp", scatter_dimension=0, tiled=True)
    text_zero = turn(model_columns(share)) + sinusoid(tokens)

    hat_three, scale_three = normalize(text_zero)
    ln_three = hat_three * norms[3, 0] + norms[3, 1]
    dec_three = mm(ln_three, dec_attn_all[:, : 3 * local])
    dec_q, dec_k, dec_v = (dec_three[:, i * local : (i + 1) * local] for i in range(3))
    dec_mixed, dec_lse = attend(dec_q, dec_k, dec_v, self_allowed)
    dec_attn = model_sum(mm_nt(dec_mixed, dec_attn_all[:, 3 * local :]))
    text_one = text_zero + dec_attn
    hat_four, scale_four = normalize(text_one)
    ln_four = hat_four * norms[4, 0] + norms[4, 1]
    cross_q = mm(ln_four, cross_all[:, :local])
    cross_mixed, cross_lse = attend(cross_q, cross_k, cross_v, frame_allowed)
    cross_attn = model_sum(mm_nt(cross_mixed, cross_all[:, 3 * local :]))
    text_two = text_one + cross_attn
    decoded, dec_pre, dec_stat = mlp_forward(
        text_two, norms[5], dec_up_all, dec_down_all, token_col, 2, "dec_mlp_forward"
    )

    def half_of(rows):
        return rows[: rows.shape[0] // 2]

    frame_weight = half_of(frame_ok).astype(jnp.float32)[:, None]
    token_weight = half_of(token_ok).astype(jnp.float32)[:, None]

    def squares(rows, weight):
        kept = half_of(rows)
        return jnp.sum(kept * kept * weight)

    local_sums = jnp.stack(
        [squares(x, frame_weight) for x in (stream_zero, enc_attn)]
        + [jnp.sum(enc_stat[0]), jnp.sum(enc_stat[1])]
        + [squares(x, token_weight) for x in (text_zero, dec_attn, cross_attn)]
        + [jnp.sum(dec_stat[0]), jnp.sum(dec_stat[1])]
    )
    local_sums = local_sums + exchange(local_sums, "mp", 1)
    square_sums = data_sum(local_sums)
    frame_total = jnp.sum((frame_mask > 0).astype(jnp.float32))
    token_total = jnp.sum((token_mask > 0).astype(jnp.float32))
    counts = jnp.concatenate([jnp.full((4,), frame_total), jnp.full((5,), token_total)])
    rms_stats = jnp.sqrt(square_sums / (counts * width))

    def norm_grads(grad, xhat):
        kept = half_of(grad)
        return jnp.stack([jnp.sum(kept * half_of(xhat), axis=0), jnp.sum(kept, axis=0)])

    def block(grad):
        return grad.reshape(n_dp, grad.shape[0] // n_dp, grad.shape[1])

    grad_text_two, grad_up, grad_down, norm_five = mlp_backward(
        cot, text_two, norms[5], dec_pre, dec_up_all, dec_down_all, 3, "dec_mlp_backward"
    )
    grad_dec_up = scatter_slow(block(grad_up))
    grad_dec_down = scatter_slow(block(grad_down))
    norm_five = norm_five[:2]

    grad_cross_out = mm_tn(grad_text_two, cross_mixed)
    grad_cq, grad_ck, grad_cv = attend_back(
        cross_q,
        cross_k,
        cross_v,
        frame_allowed,
        cross_mixed,
        cross_lse,
        mm(grad_text_two, cross_all[:, 3 * local :]),
    )
    grad_ckv = jnp.concatenate([grad_ck, grad_cv], axis=1)
    grad_cross = scatter_slow(
        block(
            jnp.concatenate([mm_tn(ln_four, grad_cq), mm_tn(memory, grad_ckv), grad_cross_out], axis=1)
        )
    )
    grad_memory = model_sum(mm_nt(grad_ckv, cross_all[:, local : 3 * local]))
    grad_ln = model_sum(mm_nt(grad_cq, cross_all[:, :local]))
    norm_four = norm_grads(grad_ln, hat_four)
    grad_text_one = grad_text_two + norm_back(grad_ln, hat_four, scale_four, norms[4, 0])

    grad_dec_out = mm_tn(grad_text_one, dec_mixed)
    grad_three = jnp.concatenate(
        attend_back(
            dec_q,
            dec_k,
            dec_v,
            self_allowed,
            dec_mixed,
            dec_lse,
            mm(grad_text_one, dec_attn_all[:, 3 * local :]),
        ),
        axis=1,
    )
    grad_dec_attn = scatter_data(
        block(jnp.concatenate([mm_tn(ln_three, grad_three), grad_dec_out], axis=1))
    )
    grad_ln = model_sum(mm_nt(grad_three, dec_attn_all[:, : 3 * local]))
    norm_three = norm_grads(grad_ln, hat_three)
    grad_text_zero = grad_text_one + norm_back(grad_ln, hat_three, scale_three, norms[3, 0])
    grad_share = lax.dynamic_slice_in_dim(turn(grad_text_zero), mp_place * embed_width, embed_width, 1)
    grad_rows = lax.all_gather(grad_share, "dp", axis=0, tiled=True)
    grad_embedding = (
        jnp.zeros(embedding.shape, jnp.float32)
        .at[safe_ids]
        .add(jnp.where(owned[:, None], grad_rows, 0.0))
    )

    norm_two = norm_grads(grad_memory, hat_two)
    grad_stream_two = norm_back(grad_memory, hat_two, scale_two, norms[2, 0])
    grad_stream_one, grad_up, grad_down, norm_one = mlp_backward(
        grad_stream_two, stream_one, norms[1], enc_pre, enc_up_all, enc_down_all, 4, "enc_mlp_backward"
    )
    grad_enc_up = scatter_data(block(grad_up))
    grad_enc_down = scatter_slow(block(grad_down))
    norm_one = norm_one[:2]

    grad_enc_out = mm_tn(grad_stream_one, enc_mixed)
    grad_three = jnp.concatenate(
        attend_back(
            enc_q,
            enc_k,
            enc_v,
            frame_allowed,
            enc_mixed,
            enc_lse,
            mm(grad_stream_one, enc_attn_all[:, 3 * local :]),
        ),
        axis=1,
    )
    grad_enc_attn = scatter_data(
        block(jnp.concatenate([mm_tn(ln_zero, grad_three), grad_enc_out], axis=1))
    )
    grad_ln = model_sum(mm_nt(grad_three, enc_attn_all[:, : 3 * local]))
    norm_zero = norm_grads(grad_ln, hat_zero)
    grad_stream_zero = grad_stream_one + norm_back(grad_ln, hat_zero, scale_zero, norms[0, 0])

    grad_stem = grad_stream_zero * gelu_slope(stem_sum)
    grad_w_two = mm_tn(stem_cat, grad_stem)
    grad_cat = mm_nt(grad_stem, w_two)
    grad_back = jnp.roll(jnp.where(first, 0.0, grad_cat[:, :stem_width]), -1, axis=0)
    grad_one = jnp.concatenate(
        [grad_cat[:, stem_width : 2 * stem_width], grad_cat[:, 2 * stem_width :] + grad_back], axis=1
    )
    grad_pre = grad_one * gelu_slope(pre_one)
    grad_both = mm_tn(grad_pre, window)
    grad_w_one = grad_both[:stem_width, : taps * mel] + grad_both[stem_width:, mel:]
    grad_window = mm(grad_pre, w_both)
    grad_mel = grad_window[:, mel : 3 * mel] + jnp.concatenate(
        [
            jnp.roll(jnp.where(last, 0.0, grad_window[:, 3 * mel :]), 1, axis=0),
            jnp.roll(jnp.where(first, 0.0, grad_window[:, :mel]), -1, axis=0),
        ],
        axis=1,
    )
    grad_mel = turn(model_sum(grad_mel)).reshape(mel_frames.shape)

    norm_all = jnp.stack([norm_zero, norm_one, norm_two, norm_three, norm_four, norm_five])
    norm_all = norm_all + exchange(norm_all, "mp", 1)
    norm_blocks = norm_all.reshape(12, n_dp, part).transpose(1, 0, 2).reshape(n_dp, -1)
    one_blocks = grad_w_one.reshape(n_dp, one_size)

    def lay(flat):
        short = -flat.shape[1] % width
        return jnp.pad(flat, ((0, 0), (0, short))).reshape(n_dp, -1, width)

    two_blocks = (
        grad_w_two.reshape(taps, n_dp, chans, width).transpose(1, 0, 2, 3).reshape(n_dp, -1, width)
    )
    stem_blocks = jnp.concatenate([two_blocks, lay(one_blocks), lay(norm_blocks)], axis=1)
    stem_blocks = jnp.pad(stem_blocks, ((0, 0), (0, -stem_blocks.shape[1] % 8), (0, 0)))
    stem_grads = scatter_data(stem_blocks)
    grad_conv_two = stem_grads[:two_rows].reshape(taps, chans, width)
    grad_conv_one = (
        stem_grads[two_rows : two_rows + one_rows]
        .reshape(-1)[:one_size]
        .reshape(chans, taps, mel)
        .transpose(1, 2, 0)
    )
    grad_norms = stem_grads[two_rows + one_rows :].reshape(-1)[: 12 * part].reshape(6, 2, part)

    def three(grads):
        return jnp.stack([grads[:, i * local : (i + 1) * local] for i in range(3)])

    return (
        turn(decoded),
        grad_mel,
        grad_embedding,
        grad_conv_one,
        grad_conv_two,
        three(grad_enc_attn),
        grad_enc_attn[:, 3 * local :].T,
        grad_enc_up,
        grad_enc_down.T,
        three(grad_cross),
        grad_cross[:, 3 * local :].T,
        three(grad_dec_attn),
        grad_dec_attn[:, 3 * local :].T,
        grad_dec_up,
        grad_dec_down.T,
        grad_norms,
        rms_stats,
    )


def solution(mesh):
    placed = (
        P("dp", None),
        P(),
        P(),
        P(),
        P("dp", "mp"),
        P(None, None, ("dp", "mp")),
        P(None, ("dp", "mp"), None),
        P(None, "dp", "mp"),
        P("mp", "dp"),
        P("dp", "mp"),
        P("mp", "dp"),
        P(None, "dp", "mp"),
        P("mp", "dp"),
        P(None, "dp", "mp"),
        P("mp", "dp"),
        P("dp", "mp"),
        P("mp", "dp"),
        P(None, None, "dp"),
        P("dp", None),
    )
    return jax.shard_map(
        body,
        mesh=mesh,
        in_specs=placed,
        out_specs=(
            P("dp", None),
            P("dp", None),
            P("dp", "mp"),
            P(None, None, ("dp", "mp")),
            P(None, ("dp", "mp"), None),
            P(None, "dp", "mp"),
            P("mp", "dp"),
            P("dp", "mp"),
            P("mp", "dp"),
            P(None, "dp", "mp"),
            P("mp", "dp"),
            P(None, "dp", "mp"),
            P("mp", "dp"),
            P("dp", "mp"),
            P("mp", "dp"),
            P(None, None, "dp"),
            P(),
        ),
        check_vma=False,
    )
```
